32 devices in a mesh: groups: 2 (over y), seq: 16 (over z, x, core).
Axes of the slice: x: 2, y: 2, z: 4, core: 2. Of those that a mesh axis runs over, the one named last changes fastest.
Arguments:
- queries: bfloat16 [8192, 2048], P(('groups', 'seq')), parts along dimension 0, may hold values from -128 to 128
- keys: bfloat16 [32768, 1024], P(('groups', 'seq')), parts along dimension 0, may hold values from -6 to 6
- values: bfloat16 [32768, 1024], P(('groups', 'seq')), parts along dimension 0, may hold values from -6 to 6
- dirty: int32 [32], P(('groups', 'seq')), parts along dimension 0, may hold values from -1 to 3
- spans: int32 [32, 2], P(('groups', 'seq')), parts along dimension 0, may hold values from 0 to 16384, as said below
Outputs:
- attended: bfloat16 [8192, 2048], P(('groups', 'seq')), parts along dimension 0
The draws below stay inside these ranges and needn't reach their ends.
There are 2 independent parts, one for each index of `groups`. The reference program is written for one: setup_inputs(seed, part) draws one part's arguments, and reference() takes and returns one part's arrays. A program takes and returns all parts, laid end to end along the dimension named above; each array names one. Nothing has to cross between parts.
Inputs may be any that keep to these rules, and one draw needn't show every extreme that they name: -1 marks a shard with no dirty block. `spans`: row k holds the start and the exclusive end of the one tombstoned span of shard k: k * 1024 <= start < end <= (k + 1) * 1024, with end - start from 1 to 32; the last shard's span has exactly 32 rows.
All inputs are finite; a program needn't handle non-finite values.
Results may differ from the reference program's by a relative error of at most 0.014.
Values may be sent and summed in bfloat16 or wider, within the bound.
No kernel may reach another device: no remote copies, remote signals or barrier semaphores. Data moves between devices by JAX's collectives and lax.ppermute only.
A program may use at most 128 MiB of HBM per device.

```python
import math
import jax
import jax.numpy as jnp
from jax import lax

QUERY_HEADS = 16
KEY_VALUE_HEADS = 8
HEAD_DIMENSION = 128
WINDOW = 4096
BLOCK_ROWS = 256
SPAN = 32
SHARD_TOKENS = 1024
DOCUMENT_LENGTH = 16384
BLK_DEV = 4
SHARDS_BACK = 5
N_SEQ = 16


def draw_spans(key, part):
    count = N_SEQ
    index = jnp.arange(count, dtype=jnp.int32)
    lowest = max(SPAN // 3, 1)
    limit = jnp.maximum(1, lowest + (SPAN - lowest) * index // max(count - 1, 1))
    key_len, key_off = jax.random.split(jax.random.fold_in(key, 11))
    length = jax.random.randint(key_len, (count,), 1, limit + 1)
    length = jnp.where(index == count - 1, SPAN, length)
    offset = jax.random.randint(key_off, (count,), 0, SHARD_TOKENS - length + 1)
    start = index * SHARD_TOKENS + offset
    return jnp.stack([start, start + length], axis=1).astype(jnp.int32)


def draw_queries(key, part):
    count = N_SEQ * BLOCK_ROWS
    key_base, key_pick = jax.random.split(jax.random.fold_in(key, 23), 2)
    pick = jax.random.randint(key_pick, (count, 1), 0, 8)
    base = jnp.clip(jax.random.normal(key_base, (count, QUERY_HEADS * HEAD_DIMENSION), jnp.float32), -4.0, 4.0)
    factor = jnp.where(pick == 0, jnp.float32(32.0), jnp.float32(1.0))
    return (base * factor).astype(jnp.bfloat16)


def set_ends(array, own_key, smallest, high):
    extent = array.shape
    spot = [jax.random.randint(jax.random.fold_in(own_key, axis), (), 0, extent[axis]) for axis in range(len(extent))]
    array = array.at[tuple(spot)].set(smallest)
    longest = extent.index(max(extent))
    spot[longest] = (spot[longest] + 1) % extent[longest]
    return array.at[tuple(spot)].set(high)


def steps_of(rng, extent, pieces, low, top_value):
    level, own = 1.0, jax.random.fold_in(rng, 6)
    for axis_at, blocks in pieces:
        heights = jnp.exp(jax.random.uniform(jax.random.fold_in(own, axis_at), (blocks,), jnp.float32, low / len(pieces), top_value / len(pieces)))
        level = level * jnp.repeat(heights, extent[axis_at] // blocks).reshape([-1 if axis == axis_at else 1 for axis in range(len(extent))])
    return level


def normal_values(rng, shape, width, bound, pieces=(), held_as=jnp.bfloat16):
    entries = jax.random.normal(rng, shape, jnp.float32) * width
    if len(pieces) > 0:
        entries = steps_of(rng, shape, pieces, -0.22, 0.18) * entries
    return jnp.clip(entries, min=-bound, max=bound).astype(held_as)


def setup_inputs(seed: int = 0, part: int = 0) -> dict:
    key_list = jax.random.split(jax.random.key(seed), 6)
    own_keys = jax.random.split(jax.random.fold_in(key_list[5], part), 6)
    queries = draw_queries(jax.random.fold_in(jax.random.fold_in(key_list[5], part), 71), part)
    keys = normal_values(own_keys[1], (DOCUMENT_LENGTH, KEY_VALUE_HEADS * HEAD_DIMENSION), 1.0, 6.0, ((0, 16),))
    values = normal_values(own_keys[2], (DOCUMENT_LENGTH, KEY_VALUE_HEADS * HEAD_DIMENSION), 1.0, 6.0, ((0, 16),))
    dirty = set_ends(jax.random.randint(own_keys[3], (N_SEQ,), -1, BLK_DEV), jax.random.fold_in(own_keys[3], 1), -1, BLK_DEV - 1).astype(jnp.int32)
    spans = draw_spans(jax.random.fold_in(jax.random.fold_in(key_list[5], part), 71), part)
    return {"queries": queries, "keys": keys, "values": values, "dirty": dirty, "spans": spans}


softcap_limit = 50.0
query_scale = 144.0 ** -0.5


def locate(raw, spans):
    begin = spans[:, 0]
    finish = spans[:, 1]
    offset = raw[:, None] - begin[None, :]
    before = jnp.sum(jnp.clip(offset, 0, (finish - begin)[None, :]), axis=1)
    inside = jnp.sum(((raw[:, None] >= begin[None, :]) & (raw[:, None] < finish[None, :])).astype(jnp.int32), axis=1)
    return (raw - before).astype(jnp.int32), (inside == 0) & (raw >= 0)


def apply_rotary(field, place):
    half = field.shape[-1] // 2
    order = jnp.arange(half, dtype=jnp.float32)
    freq = jnp.exp(order * (-2.0 * math.log(10000.0) / field.shape[-1]))
    angle = place[:, None] * freq[None, :]
    cosine = jnp.cos(angle)[:, None, :]
    sine = jnp.sin(angle)[:, None, :]
    first = field[..., :half]
    second = field[..., half:]
    return jnp.concatenate([first * cosine - second * sine, second * cosine + first * sine], axis=-1)


def reference(queries, keys, values, dirty, spans):
    head_group = QUERY_HEADS // KEY_VALUE_HEADS
    window_margin = SHARDS_BACK * SHARD_TOKENS
    window_width = window_margin + SHARD_TOKENS
    padded_keys = jnp.concatenate([jnp.zeros((window_margin, KEY_VALUE_HEADS * HEAD_DIMENSION), jnp.bfloat16), keys], axis=0)
    padded_values = jnp.concatenate([jnp.zeros((window_margin, KEY_VALUE_HEADS * HEAD_DIMENSION), jnp.bfloat16), values], axis=0)

    def one_shard(shard_index):
        block = dirty[shard_index]
        chosen = jnp.maximum(block, 0)
        q_raw = (shard_index * SHARD_TOKENS + chosen * BLOCK_ROWS + jnp.arange(BLOCK_ROWS)).astype(jnp.int32)
        q_pos, q_live = locate(q_raw, spans)
        q_rows = lax.dynamic_slice(queries, ((shard_index * BLOCK_ROWS).astype(jnp.int32), jnp.int32(0)), (BLOCK_ROWS, QUERY_HEADS * HEAD_DIMENSION))
        query_rotary = (apply_rotary(q_rows.astype(jnp.float32).reshape(BLOCK_ROWS, QUERY_HEADS, HEAD_DIMENSION), q_pos.astype(jnp.float32)) * query_scale).astype(jnp.bfloat16)
        query_rotary = lax.optimization_barrier(query_rotary).astype(jnp.float32).reshape(BLOCK_ROWS, KEY_VALUE_HEADS, head_group, HEAD_DIMENSION)
        k_raw = (shard_index * SHARD_TOKENS - window_margin + jnp.arange(window_width)).astype(jnp.int32)
        key_position, k_live = locate(k_raw, spans)
        key_row_block = lax.dynamic_slice(padded_keys, ((shard_index * SHARD_TOKENS).astype(jnp.int32), jnp.int32(0)), (window_width, KEY_VALUE_HEADS * HEAD_DIMENSION))
        value_row_block = lax.dynamic_slice(padded_values, ((shard_index * SHARD_TOKENS).astype(jnp.int32), jnp.int32(0)), (window_width, KEY_VALUE_HEADS * HEAD_DIMENSION))
        key_rotary = apply_rotary(key_row_block.astype(jnp.float32).reshape(window_width, KEY_VALUE_HEADS, HEAD_DIMENSION), key_position.astype(jnp.float32)).astype(jnp.bfloat16)
        key_rotary = lax.optimization_barrier(key_rotary).astype(jnp.float32)
        score = jnp.einsum('qhgd,khd->hgqk', query_rotary, key_rotary)
        capped = softcap_limit * jnp.tanh(score / softcap_limit)
        allowed = k_live[None, :] & (k_raw[None, :] <= q_raw[:, None]) & ((q_pos[:, None] - key_position[None, :]) < WINDOW)
        weight = jnp.where(allowed[None, None], jnp.exp(capped), jnp.float32(0.0))
        total = jnp.sum(weight, axis=-1)
        total = jnp.where(total > 0, total, jnp.float32(1.0))
        rounded_weight = lax.optimization_barrier(weight.astype(jnp.bfloat16)).astype(jnp.float32)
        numerator = jnp.einsum('nexi,inv->xnev', rounded_weight, value_row_block.astype(jnp.float32).reshape(window_width, KEY_VALUE_HEADS, HEAD_DIMENSION))
        result = numerator / jnp.transpose(total, (2, 0, 1))[..., None]
        keep = q_live & (block >= 0)
        result = jnp.where(keep[:, None, None, None], result, jnp.float32(0.0))
        return result.reshape(BLOCK_ROWS, QUERY_HEADS * HEAD_DIMENSION).astype(jnp.bfloat16)

    blocks = lax.map(one_shard, jnp.arange(N_SEQ, dtype=jnp.int32))
    return blocks.reshape(N_SEQ * BLOCK_ROWS, QUERY_HEADS * HEAD_DIMENSION)
```

```python
import functools
import math

import jax
import jax.numpy as jnp
import numpy as np
from jax import lax
from jax.experimental import pallas as pl
from jax.experimental.pallas import tpu as pltpu
from jax.sharding import PartitionSpec as P

HEAD_DIMENSION = 128
WINDOW = 4096
BLOCK_ROWS = 256
SPAN = 32

SOFTCAP = 50.0
QUERY_SCALE = 144.0 ** (-0.5)
TO_TANH = 1.0 / SOFTCAP
TO_EXP2 = SOFTCAP * math.log2(math.e)

HALF = HEAD_DIMENSION // 2
LANES = 128
TABLE_COLUMNS = 4


def lane_frequency():
    order = np.arange(HEAD_DIMENSION) % HALF
    return np.exp(order * (-2.0 * math.log(10000.0) / HEAD_DIMENSION)).astype(np.float32)


def row_angles():
    angle = np.arange(BLOCK_ROWS, dtype=np.float64)[:, None] * lane_frequency().astype(np.float64)[None, :]
    sign = np.where(np.arange(HEAD_DIMENSION) < HALF, -1.0, 1.0)[None, :]
    return np.stack([np.cos(angle), np.sin(angle) * sign]).astype(np.float32)


def shift(array, axis, by):
    count = lax.axis_size(axis)
    pairs = [(i, i + by) for i in range(count) if 0 <= i + by < count]
    return lax.ppermute(array, axis, pairs)


class Frame:
    def __init__(self, table, chip, rows, shards):
        self.table, self.chip, self.rows, self.shards = table, chip, rows, shards

    def span(self, shard):
        inside = (shard >= 0) & (shard < self.shards)
        at = jnp.clip(shard, 0, self.shards - 1)
        start = jnp.where(inside, self.table[at, 0] - at * self.rows, 0)
        length = jnp.where(inside, self.table[at, 1] - self.table[at, 0], 0)
        return start, length

    def tile(self, shard_step, row):
        shard = self.chip + shard_step
        start, length = self.span(shard)
        first = shard_step * self.rows + row
        for step in range(min(shard_step, 0), max(shard_step, 0)):
            _, other = self.span(self.chip + step)
            first = first - other if step >= 0 else first + other
        first = first - jnp.clip(row - start, 0, length)
        begin = start - row
        end = begin + length
        gone = jnp.clip(end, 0, BLOCK_ROWS) - jnp.clip(begin, 0, BLOCK_ROWS)
        return first, first - gone, begin, end


def wave(offsets, freq):
    count = -(-len(offsets) // 8) * 8
    row = lax.broadcasted_iota(jnp.int32, (count, LANES), 0)
    lane = lax.broadcasted_iota(jnp.int32, (count, LANES), 1)
    value = jnp.zeros((count, LANES), jnp.int32)
    for k, offset in enumerate(offsets):
        value = jnp.where(row == k, offset, value)
    angle = value.astype(jnp.float32) * freq
    sine = jnp.sin(angle)
    return jnp.cos(angle), jnp.where(lane < HALF, -sine, sine)


def rope_tables(angles, begin, waves, at, scale):
    cosine, sine = waves
    row = lax.broadcasted_iota(jnp.int32, (BLOCK_ROWS, LANES), 0)
    early = row < begin
    c = jnp.where(early, cosine[at : at + 1], cosine[at + 1 : at + 2])
    s = jnp.where(early, sine[at : at + 1], sine[at + 1 : at + 2])
    rc, rs = angles[0], angles[1]
    return (rc * c - rs * s) * scale, (rs * c + rc * s) * scale


def rotate(x, c, s):
    x = x.astype(jnp.float32)
    return (x * c + pltpu.roll(x, HALF, 1) * s).astype(jnp.bfloat16)


def places(tile, dim, shape):
    first, later, begin, end = tile
    row = lax.broadcasted_iota(jnp.int32, shape, dim)
    return row + jnp.where(row < begin, first, later)


def visit(kind, step, table, index, frame, angles, freq, query, kr, vz, lv, out, total, rot):
    rows, shards = frame.rows, frame.shards
    per = rows // BLOCK_ROWS
    kv_heads = kr.shape[0]
    shard = index + step
    at = jnp.minimum(shard, shards - 1)
    block = table[at, 2]
    valid = (shard < shards) & (block >= 0)
    block = jnp.maximum(block, 0)
    out[...] = jnp.zeros(out.shape, out.dtype)

    odd = index - frame.chip

    @pl.when(valid)
    def _():
        even_tile = frame.tile(step, block * BLOCK_ROWS)
        odd_tile = frame.tile(step + 1, block * BLOCK_ROWS)
        tile = [jnp.where(odd == 1, b, a) for a, b in zip(even_tile, odd_tile)]
        waves = wave([tile[0], tile[1]], freq)
        c, s = rope_tables(angles, tile[2], waves, 0, QUERY_SCALE)
        for head in range(2 * kv_heads):
            cols = slice(head * HEAD_DIMENSION, (head + 1) * HEAD_DIMENSION)
            rot[head] = rotate(query[:, cols], c, s)
        total[...] = jnp.zeros(total.shape, total.dtype)
        lane = lax.broadcasted_iota(jnp.int32, (BLOCK_ROWS, LANES), 1)
        own = places(tile, 0, (BLOCK_ROWS, 1))

        def run(count, begin, masked, keep):
            def one(h, carry):
                from_row = pl.multiple_of(begin * BLOCK_ROWS, BLOCK_ROWS)
                k = kr[h, pl.ds(from_row, count * BLOCK_ROWS), :]
                v = jnp.concatenate(
                    [
                        vz[h, pl.ds(from_row, count * BLOCK_ROWS), :],
                        lv[pl.ds(from_row, count * BLOCK_ROWS), :],
                    ],
                    axis=1,
                )
                for g in range(2):
                    head = 2 * h + g
                    score = lax.dot_general(
                        rot[head], k, (((1,), (1,)), ((), ())), preferred_element_type=jnp.float32
                    )
                    weight = jnp.exp2(jnp.tanh(score * TO_TANH) * TO_EXP2)
                    if keep is not None:
                        lo, hi = masked
                        parts = []
                        if lo > 0:
                            parts.append(weight[:, : lo * BLOCK_ROWS])
                        parts.append(
                            jnp.where(keep, weight[:, lo * BLOCK_ROWS : hi * BLOCK_ROWS], 0.0)
                        )
                        if hi < count:
                            parts.append(weight[:, hi * BLOCK_ROWS :])
                        weight = jnp.concatenate(parts, axis=1) if len(parts) > 1 else parts[0]
                    both = jnp.dot(
                        weight.astype(jnp.bfloat16), v, preferred_element_type=jnp.float32
                    )
                    where = pl.multiple_of(head * HEAD_DIMENSION, HEAD_DIMENSION)
                    out[:, pl.ds(where, HEAD_DIMENSION)] = both[:, :HEAD_DIMENSION].astype(jnp.bfloat16)
                    t = both[:, HEAD_DIMENSION:]
                    high = t.astype(jnp.bfloat16).astype(jnp.float32)
                    total[...] = jnp.where(
                        lane == head,
                        high,
                        jnp.where(lane == head + 2 * kv_heads, t - high, total[...]),
                    )
                return carry

            lax.fori_loop(0, kv_heads, one, 0)

        if kind == "middle":
            run(2 * per, 1, None, None)
        elif kind == "own":
            tiles = odd * per + block + 1
            for count in range(1, 2 * per + 1):

                @pl.when(tiles == count)
                def _(count=count):
                    shard_step, tile_row = (count - 1) // per, (count - 1) % per * BLOCK_ROWS
                    key = places(frame.tile(shard_step, tile_row), 1, (1, BLOCK_ROWS))
                    keep = own >= key
                    run(count, 1, (count - 1, count), keep)
        else:
            begin = odd * per + block
            for first in range(2 * per):

                @pl.when(begin == first)
                def _(first=first):
                    count = 2 * per + 1 - first
                    keys = []
                    for t in (first, first + 1):
                        shard_step, tile_row = (t - 1) // per, (t - 1) % per * BLOCK_ROWS
                        keys.append(places(frame.tile(shard_step, tile_row), 1, (1, BLOCK_ROWS)))
                    key = jnp.concatenate(keys, axis=1)
                    keep = own - key < WINDOW
                    run(count, first, (0, 2), keep)

        out[:, 2 * kv_heads * HEAD_DIMENSION :] = total[...].astype(jnp.bfloat16)


def first_kernel(
    shards, table, index_ref, angles, freq, query, k_own, k_other, v_own, v_other, tail,
    kr, vz, lv, out, total, rot,
):
    rows = k_own.shape[0]
    per = rows // BLOCK_ROWS
    reach = tail.shape[0] // 2
    kv_heads = kr.shape[0]
    index = index_ref[0]
    odd = lax.rem(index, 2)
    frame = Frame(table, index - odd, rows, shards)
    steps = [(-1, per - 1)] + [(s, t) for s in (0, 1) for t in range(per)]
    tiles = [frame.tile(s, t * BLOCK_ROWS) for s, t in steps]
    waves = wave([o for tile in tiles for o in tile[:2]], freq[...])
    row = lax.broadcasted_iota(jnp.int32, (BLOCK_ROWS, LANES), 0)

    def prepare(at, load_k, load_v, fresh):
        tile = tiles[at]
        c, s = rope_tables(angles, tile[2], waves, 2 * at, 1.0)
        live = (row < tile[2]) | (row >= tile[3])
        if fresh:
            live = live & (row >= fresh) & (odd == 0) & (frame.chip > 0)
        into = slice(at * BLOCK_ROWS, (at + 1) * BLOCK_ROWS)
        lv[into, :] = jnp.where(live, 1.0, 0.0).astype(jnp.bfloat16)
        for h in range(kv_heads):
            cols = slice(h * HEAD_DIMENSION, (h + 1) * HEAD_DIMENSION)
            kr[h, into, :] = rotate(load_k(cols), c, s)
            vz[h, into, :] = jnp.where(live, load_v(cols).astype(jnp.float32), 0.0).astype(jnp.bfloat16)

    def padded(ref, low, cols):
        zero = jnp.zeros((BLOCK_ROWS - reach, HEAD_DIMENSION), ref.dtype)
        return jnp.concatenate([zero, ref[low : low + reach, cols]], axis=0)

    prepare(
        0,
        lambda cols: padded(tail, 0, cols),
        lambda cols: padded(tail, reach, cols),
        BLOCK_ROWS - reach,
    )
    for shard in (0, 1):
        for mine, k_ref, v_ref in ((True, k_own, v_own), (False, k_other, v_other)):

            @pl.when((odd == shard) == mine)
            def _(shard=shard, k_ref=k_ref, v_ref=v_ref):
                for t in range(per):
                    rows_of = slice(t * BLOCK_ROWS, (t + 1) * BLOCK_ROWS)
                    prepare(
                        1 + shard * per + t,
                        lambda cols, r=rows_of: k_ref[r, cols],
                        lambda cols, r=rows_of: v_ref[r, cols],
                        0,
                    )

    visit("own", 0, table, index, frame, angles, freq[...], query, kr, vz, lv, out, total, rot)


def visit_kernel(kind, step, shards, rows, table, index_ref, angles, freq, query, kr, vz, lv, out, total, rot):
    index = index_ref[0]
    frame = Frame(table, index - lax.rem(index, 2), rows, shards)
    visit(kind, step, table, index, frame, angles, freq[...], query, kr, vz, lv, out, total, rot)


def last_kernel(rows, table, index_ref, a, b, c, out):
    index = index_ref[0]
    heads = out.shape[1] // HEAD_DIMENSION
    width = out.shape[1]
    block = table[index, 2]
    first = index * rows + jnp.maximum(block, 0) * BLOCK_ROWS
    row = lax.broadcasted_iota(jnp.int32, (BLOCK_ROWS, LANES), 0) + first
    keep = ((row < table[index, 0]) | (row >= table[index, 1])) & (block >= 0)
    totals = jnp.concatenate([p[:, width:] for p in (a, b, c)], axis=1)
    line = lax.rem(lax.broadcasted_iota(jnp.int32, (3 * LANES, LANES), 0), LANES)
    for head in range(heads):
        pick = jnp.where((line == head) | (line == head + heads), 1.0, 0.0).astype(jnp.bfloat16)
        total = jnp.dot(totals, pick, preferred_element_type=jnp.float32)
        total = jnp.where(total > 0, total, 1.0)
        cols = slice(head * HEAD_DIMENSION, (head + 1) * HEAD_DIMENSION)
        number = (
            a[:, cols].astype(jnp.float32) + b[:, cols].astype(jnp.float32) + c[:, cols].astype(jnp.float32)
        )
        out[:, cols] = jnp.where(keep, number / total, 0.0).astype(out.dtype)


SMEM = pl.BlockSpec(memory_space=pltpu.SMEM)
VMEM = pl.BlockSpec(memory_space=pltpu.VMEM)


def body(queries, keys, values, dirty, spans):
    shards = lax.axis_size("seq")
    index = lax.axis_index("seq")
    rows, columns = keys.shape
    kv_heads = columns // HEAD_DIMENSION
    q_heads = queries.shape[1] // HEAD_DIMENSION
    per = rows // BLOCK_ROWS
    back = WINDOW // rows
    reach = (back + 1) * SPAN
    swap = [(i, i ^ 1) for i in range(shards)]

    mine = jnp.concatenate([spans[0], dirty, jnp.zeros((1,), jnp.int32)])
    sits = (jnp.arange(shards) == index)[:, None]
    table = lax.psum(jnp.where(sits, mine[None, :], 0), "seq")

    k_other = lax.ppermute(keys, "seq", swap)
    v_other = lax.ppermute(values, "seq", swap)
    far = shift(queries, "seq", -back)
    near = shift(queries, "seq", -back // 2)
    tail = lax.ppermute(
        jnp.concatenate([keys[rows - reach :], values[rows - reach :]]),
        "seq",
        [(i, i + 1) for i in range(1, shards - 1, 2)],
    )

    at = index.astype(jnp.int32).reshape(1)
    angles = jnp.asarray(row_angles())
    freq = jnp.asarray(lane_frequency()[None, :])
    tiles = 2 * per + 1
    payload = jax.ShapeDtypeStruct((BLOCK_ROWS, q_heads * HEAD_DIMENSION + LANES), jnp.bfloat16)
    by_head = jax.ShapeDtypeStruct((kv_heads, tiles * BLOCK_ROWS, HEAD_DIMENSION), jnp.bfloat16)
    scratch = [
        pltpu.VMEM((BLOCK_ROWS, LANES), jnp.float32),
        pltpu.VMEM((q_heads, BLOCK_ROWS, HEAD_DIMENSION), jnp.bfloat16),
    ]
    params = pltpu.CompilerParams(vmem_limit_bytes=48 << 20)
    kr, vz, lv, own = pl.pallas_call(
        functools.partial(first_kernel, shards),
        out_shape=(
            by_head,
            by_head,
            jax.ShapeDtypeStruct((tiles * BLOCK_ROWS, LANES), jnp.bfloat16),
            payload,
        ),
        in_specs=[SMEM, SMEM] + [VMEM] * 8,
        out_specs=[VMEM] * 4,
        scratch_shapes=scratch,
        compiler_params=params,
        name="first",
    )(table, at, angles, freq, queries, keys, k_other, values, v_other, tail)

    def visitor(kind, step, query):
        return pl.pallas_call(
            functools.partial(visit_kernel, kind, step, shards, rows),
            out_shape=payload,
            in_specs=[SMEM, SMEM] + [VMEM] * 6,
            out_specs=VMEM,
            scratch_shapes=scratch,
            compiler_params=params,
            name=kind,
        )(table, at, angles, freq, query, kr, vz, lv)

    near_part = shift(visitor("middle", back // 2, near), "seq", back // 2)
    far_part = shift(visitor("window", back, far), "seq", back)
    return pl.pallas_call(
        functools.partial(last_kernel, rows),
        out_shape=jax.ShapeDtypeStruct(queries.shape, queries.dtype),
        in_specs=[SMEM, SMEM] + [VMEM] * 3,
        out_specs=VMEM,
        compiler_params=params,
        name="last",
    )(table, at, own, near_part, far_part)


def solution(mesh):
    placed = (
        P(("groups", "seq"), None),
        P(("groups", "seq"), None),
        P(("groups", "seq"), None),
        P(("groups", "seq")),
        P(("groups", "seq"), None),
    )
    return jax.shard_map(
        body, mesh=mesh, in_specs=placed, out_specs=P(("groups", "seq"), None), check_vma=False
    )
```

```python
import functools
import math

import jax
import jax.numpy as jnp
import numpy as np
from jax import lax
from jax.experimental import pallas as pl
from jax.experimental.pallas import tpu as pltpu
from jax.sharding import PartitionSpec as P


HEAD_DIMENSION = 128
WINDOW = 4096
BLOCK_ROWS = 256
SPAN = 32

SOFTCAP = 50.0
QUERY_SCALE = 144.0 ** (-0.5)
TO_TANH = 1.0 / SOFTCAP
TO_EXP2 = SOFTCAP * math.log2(math.e)

HALF = HEAD_DIMENSION // 2
LANES = 128
NOTE_ROWS = 8
DIGIT = 32
VMEM_LIMIT = 32 << 20


def lane_frequency():
    order = np.arange(HEAD_DIMENSION) % HALF
    return np.exp(order * (-2.0 * math.log(10000.0) / HEAD_DIMENSION)).astype(np.float32)


def row_angles():
    angle = np.arange(BLOCK_ROWS, dtype=np.float64)[:, None] * lane_frequency().astype(np.float64)[None, :]
    sign = np.where(np.arange(HEAD_DIMENSION) < HALF, -1.0, 1.0)[None, :]
    return np.stack([np.cos(angle), np.sin(angle) * sign]).astype(np.float32)


def send(array, pairs):
    return lax.ppermute(array, "seq", pairs)


def shift(array, by):
    count = lax.axis_size("seq")
    return send(array, [(i, i + by) for i in range(count) if 0 <= i + by < count])


class Frame:
    def __init__(self, spans, rows):
        self.spans, self.rows = spans, rows

    def tile(self, shard_step, row):
        start, length = self.spans[shard_step]
        first = shard_step * self.rows + row
        for step in range(min(shard_step, 0), max(shard_step, 0)):
            _, other = self.spans[step]
            first = first - other if step >= 0 else first + other
        first = first - jnp.clip(row - start, 0, length)
        begin = start - row
        end = begin + length
        gone = jnp.clip(end, 0, BLOCK_ROWS) - jnp.clip(begin, 0, BLOCK_ROWS)
        return first, first - gone, begin, end


def by_parity(odd, mine, other):
    mine = [jnp.where(odd == 1, b, a) for a, b in zip(mine, other)], [
        jnp.where(odd == 1, a, b) for a, b in zip(mine, other)
    ]
    return mine


def write_note(ref, numbers):
    shape = (NOTE_ROWS, ref.shape[1])
    lane = lax.broadcasted_iota(jnp.int32, shape, 1)
    row = jnp.zeros(shape, jnp.int32)
    for k, number in enumerate(numbers):
        row = jnp.where(lane == 2 * k, number // DIGIT, jnp.where(lane == 2 * k + 1, number % DIGIT, row))
    ref[ref.shape[0] - NOTE_ROWS :, :] = row.astype(jnp.float32).astype(jnp.bfloat16)


def read_note(ref, count):
    low = ref[ref.shape[0] - NOTE_ROWS :, :LANES].astype(jnp.float32)
    shape = (NOTE_ROWS, LANES)
    lane = lax.broadcasted_iota(jnp.int32, shape, 1)
    first = lax.broadcasted_iota(jnp.int32, shape, 0) == 0
    out = []
    for k in range(count):
        digits = jnp.where(lane == 2 * k, low * DIGIT, jnp.where(lane == 2 * k + 1, low, 0.0))
        out.append(jnp.sum(jnp.where(first, digits, 0.0)).astype(jnp.int32))
    return out


def wave(offsets, freq):
    count = -(-len(offsets) // 8) * 8
    row = lax.broadcasted_iota(jnp.int32, (count, LANES), 0)
    lane = lax.broadcasted_iota(jnp.int32, (count, LANES), 1)
    value = jnp.zeros((count, LANES), jnp.int32)
    for k, offset in enumerate(offsets):
        value = jnp.where(row == k, offset, value)
    angle = value.astype(jnp.float32) * freq
    sine = jnp.sin(angle)
    return jnp.cos(angle), jnp.where(lane < HALF, -sine, sine)


def rope_tables(angles, begin, waves, at, scale):
    cosine, sine = waves
    row = lax.broadcasted_iota(jnp.int32, (BLOCK_ROWS, LANES), 0)
    early = row < begin
    c = jnp.where(early, cosine[at : at + 1], cosine[at + 1 : at + 2])
    s = jnp.where(early, sine[at : at + 1], sine[at + 1 : at + 2])
    rc, rs = angles[0], angles[1]
    return (rc * c - rs * s) * scale, (rs * c + rc * s) * scale


def rotate(x, c, s):
    x = x.astype(jnp.float32)
    return (x * c + pltpu.roll(x, HALF, 1) * s).astype(jnp.bfloat16)


def places(tile, dim, shape):
    first, later, begin, _ = tile
    row = lax.broadcasted_iota(jnp.int32, shape, dim)
    return row + jnp.where(row < begin, first, later)


def visit(kind, index, block, frame, freq, angles, part, query, keys, edge, out, scratch):
    kr, vz, lv = keys
    _, rot, acc, ke, ve, le = scratch
    odd = lax.rem(index, 2)
    per = frame.rows // BLOCK_ROWS
    q_heads = acc.shape[0]
    kv_heads = q_heads // 2
    low = part * kv_heads
    pair = [frame.tile(s, block * BLOCK_ROWS) for s in edge["block"]]
    tile = [jnp.where(odd == 1, b, a) for a, b in zip(*pair)]
    waves = wave([tile[0], tile[1]], freq)
    c, s = rope_tables(angles, tile[2], waves, 0, QUERY_SCALE)
    for head in range(q_heads):
        cols = slice(head * HEAD_DIMENSION, (head + 1) * HEAD_DIMENSION)
        rot[head] = rotate(query[:BLOCK_ROWS, cols], c, s)
    own = places(tile, 0, (BLOCK_ROWS, 1))

    def add(head, keys_of, values_of, keep, fresh):
        score = lax.dot_general(
            rot[head], keys_of, (((1,), (1,)), ((), ())), preferred_element_type=jnp.float32
        )
        weight = jnp.exp2(jnp.tanh(score * TO_TANH) * TO_EXP2)
        if keep is not None:
            weight = jnp.where(keep, weight, 0.0)
        both = jnp.dot(weight.astype(jnp.bfloat16), values_of, preferred_element_type=jnp.float32)
        acc[head] = both if fresh else acc[head] + both

    def many(begin, count, fresh):
        some = pl.ds(pl.multiple_of(begin * BLOCK_ROWS, BLOCK_ROWS), count * BLOCK_ROWS)

        def one(i, carry):
            v = jnp.concatenate([vz[low + i, some, :], lv[some, :]], axis=1)
            for g in range(2):
                add(2 * i + g, kr[low + i, some, :], v, None, fresh)
            return carry

        lax.fori_loop(0, kv_heads, one, 0)

    def single(at, carry):
        some = pl.ds(pl.multiple_of(at * BLOCK_ROWS, BLOCK_ROWS), BLOCK_ROWS)
        live = lv[some, :]
        for i in range(kv_heads):
            v = jnp.concatenate([vz[low + i, some, :], live], axis=1)
            for g in range(2):
                add(2 * i + g, kr[low + i, some, :], v, None, False)
        return carry

    def stage(slot, at):
        some = pl.ds(pl.multiple_of(at * BLOCK_ROWS, BLOCK_ROWS), BLOCK_ROWS)
        for i in range(kv_heads):
            ke[slot, i] = kr[low + i, some, :]
            ve[slot, i] = vz[low + i, some, :]
        le[slot] = lv[some, :]

    def masked(slot, keep, fresh):
        for i in range(kv_heads):
            v = jnp.concatenate([ve[slot, i], le[slot]], axis=1)
            for g in range(2):
                add(2 * i + g, ke[slot, i], v, keep, fresh)

    def places_at(at):
        pair = [frame.tile(s, at * BLOCK_ROWS) for s in (0, 1)]
        tile = [jnp.where(odd == 1, b, a) for a, b in zip(*pair)]
        return places(tile, 1, (1, BLOCK_ROWS))

    if kind == "middle":
        many(0, 2 * per, True)
    elif kind == "own":
        stage(0, odd * per + block)
        masked(0, own >= places_at(block), True)

        @pl.when(odd == 1)
        def _():
            many(0, per, False)

        lax.fori_loop(odd * per, odd * per + block, single, 0)
    else:
        first = odd * per + block
        tail_k, tail_v, tail_tile = edge["tail"]

        @pl.when(first > 0)
        def _():
            stage(0, first - 1)

        @pl.when(first == 0)
        def _():
            reach = tail_k.shape[0]
            row = lax.broadcasted_iota(jnp.int32, (BLOCK_ROWS, LANES), 0)
            live = (row < tail_tile[2]) | (row >= tail_tile[3])
            live = live & (row >= BLOCK_ROWS - reach) & (index > 0)
            c, s = rope_tables(angles, tail_tile[2], wave(list(tail_tile[:2]), freq), 0, 1.0)
            le[0] = jnp.where(live, 1.0, 0.0).astype(jnp.bfloat16)
            zero = jnp.zeros((BLOCK_ROWS - reach, HEAD_DIMENSION), jnp.bfloat16)
            for i in range(kv_heads):
                at = pl.multiple_of((low + i) * HEAD_DIMENSION, HEAD_DIMENSION)
                cols = pl.ds(at, HEAD_DIMENSION)
                ke[0, i] = rotate(jnp.concatenate([zero, tail_k[:, cols]], axis=0), c, s)
                ve[0, i] = jnp.concatenate([zero, tail_v[:, cols]], axis=0) * le[0]

        stage(1, first)
        before = places_at(block - 1)
        before = jnp.where(first == 0, places(tail_tile, 1, (1, BLOCK_ROWS)), before)
        masked(0, own - before < WINDOW, True)
        masked(1, own - places_at(block) < WINDOW, False)

        @pl.when(odd == 0)
        def _():
            many(per, per, False)

        lax.fori_loop(first + 1, (odd + 1) * per, single, 0)

    lane = lax.broadcasted_iota(jnp.int32, (BLOCK_ROWS, LANES), 1)
    sums = jnp.zeros((BLOCK_ROWS, LANES), jnp.float32)
    for head in range(q_heads):
        cols = slice(head * HEAD_DIMENSION, (head + 1) * HEAD_DIMENSION)
        out[:, cols] = acc[head, :, :HEAD_DIMENSION].astype(jnp.bfloat16)
        t = acc[head, :, HEAD_DIMENSION:]
        high = t.astype(jnp.bfloat16).astype(jnp.float32)
        sums = jnp.where(lane == head, high, jnp.where(lane == head + q_heads, t - high, sums))
    out[:, q_heads * HEAD_DIMENSION :] = sums.astype(jnp.bfloat16)


def pack_kernel(spans, other, dirty, keys, values, query, *refs):
    parts = refs[:-2]
    tail, sem = refs[-2:]
    rows = keys.shape[0]
    width = parts[0].shape[1]
    reach = (tail.shape[0] - NOTE_ROWS) // 2
    copies = [
        (query.at[:, p * width : (p + 1) * width], part.at[:BLOCK_ROWS]) for p, part in enumerate(parts)
    ]
    copies += [
        (keys.at[rows - reach :], tail.at[:reach]),
        (values.at[rows - reach :], tail.at[reach : 2 * reach]),
    ]
    copies = [pltpu.make_async_copy(a, b, sem.at[k]) for k, (a, b) in enumerate(copies)]
    for copy in copies:
        copy.start()
    mine = [lax.rem(spans[0, 0], rows), spans[0, 1] - spans[0, 0]]
    write_note(
        parts[0], mine + [lax.rem(other[0, 0], rows), other[0, 1] - other[0, 0], dirty[0] + 1]
    )
    write_note(tail, mine)
    for copy in copies:
        copy.wait()


def chip_spans(index, rows, spans, other):
    mine = [lax.rem(spans[0, 0], rows), spans[0, 1] - spans[0, 0]]
    others = [lax.rem(other[0, 0], rows), other[0, 1] - other[0, 0]]
    return by_parity(lax.rem(index, 2), mine, others)


def prepare_kernel(
    index_ref, spans, other, angles, freq, k_own, k_other, v_own, v_other, kr, vz, lv, kb, vb, waves, sem,
):
    rows = k_own.shape[0]
    per = rows // BLOCK_ROWS
    kv_heads = kr.shape[0]
    index = index_ref[0]
    odd = lax.rem(index, 2)

    def copies(i, pair):
        into = pl.ds(pl.multiple_of(i * BLOCK_ROWS, BLOCK_ROWS), BLOCK_ROWS)
        t = lax.rem(i, per)
        of = pl.ds(pl.multiple_of(t * BLOCK_ROWS, BLOCK_ROWS), BLOCK_ROWS)
        return [
            pltpu.make_async_copy(ref.at[of, :], buf.at[into, :], sem.at[k, i])
            for k, (ref, buf) in enumerate(zip(pair, (kb, vb)))
        ]

    for i in range(2 * per):
        for copy in copies(i, (k_own, v_own) if i < per else (k_other, v_other)):
            copy.start()
    frame = Frame(dict(enumerate(chip_spans(index, rows, spans, other))), rows)
    tiles = [frame.tile(s, t * BLOCK_ROWS) for s in (0, 1) for t in range(per)]
    waves[0], waves[1] = wave([o for tile in tiles for o in tile[:2]], freq[...])
    row = lax.broadcasted_iota(jnp.int32, (BLOCK_ROWS, LANES), 0)

    def one(i, carry):
        for copy in copies(i, (k_own, v_own)):
            copy.wait()
        shard = jnp.where(i < per, odd, 1 - odd)
        t = lax.rem(i, per)
        at = shard * per + t
        tile = [
            jnp.where(shard == 1, b, a)
            for a, b in zip(*[frame.tile(s, t * BLOCK_ROWS) for s in (0, 1)])
        ]
        rows_of = (waves[0, pl.ds(2 * at, 2), :], waves[1, pl.ds(2 * at, 2), :])
        c, s = rope_tables(angles, tile[2], rows_of, 0, 1.0)
        live = jnp.where((row < tile[2]) | (row >= tile[3]), 1.0, 0.0).astype(jnp.bfloat16)
        into = pl.ds(pl.multiple_of(at * BLOCK_ROWS, BLOCK_ROWS), BLOCK_ROWS)
        of = pl.ds(pl.multiple_of(i * BLOCK_ROWS, BLOCK_ROWS), BLOCK_ROWS)
        lv[into, :] = live
        for h in range(kv_heads):
            cols = slice(h * HEAD_DIMENSION, (h + 1) * HEAD_DIMENSION)
            kr[h, into, :] = rotate(kb[of, cols], c, s)
            vz[h, into, :] = vb[of, cols] * live
        return carry

    lax.fori_loop(0, 2 * per, one, 0)


def visit_kernel(kind, step, shards, rows, index_ref, part_ref, spans, other, dirty, *refs):
    notes, refs = refs[: step // 2], refs[step // 2 :]
    if kind == "window":
        tail, refs = refs[0], refs[1:]
    angles, freq, kr, vz, lv, queries, out = refs[:7]
    scratch = refs[7:]
    index, part = index_ref[0], part_ref[0]
    odd = lax.rem(index, 2)
    held = dict(enumerate(chip_spans(index, rows, spans, other)))
    block = dirty[0]
    for chip, note in enumerate(notes, 1):
        note = read_note(note, 5)
        held[2 * chip], held[2 * chip + 1] = by_parity(odd, note[:2], note[2:4])
        block = note[4] - 1
    valid = (index + step < shards) & (block >= 0)
    out[...] = jnp.zeros(out.shape, out.dtype)

    @pl.when(valid)
    def _():
        edge = {"block": (step, step + 1)}
        if kind == "window":
            held[-1] = read_note(tail, 2)
            reach = (tail.shape[0] - NOTE_ROWS) // 2
            tail_tile = Frame(held, rows).tile(-1, rows - BLOCK_ROWS)
            edge["tail"] = tail.at[:reach, :], tail.at[reach : 2 * reach, :], tail_tile
        frame = Frame(held, rows)
        keys = (kr, vz, lv)
        visit(kind, index, block, frame, freq[...], angles, part, queries, keys, edge, out, scratch)


def last_kernel(rows, parts, spans, dirty, index_ref, *refs):
    out = refs[-1]
    index = index_ref[0]
    heads = out.shape[1] // HEAD_DIMENSION // parts
    width = heads * HEAD_DIMENSION
    block = dirty[0]
    first = index * rows + jnp.maximum(block, 0) * BLOCK_ROWS
    row = lax.broadcasted_iota(jnp.int32, (BLOCK_ROWS, LANES), 0) + first
    keep = ((row < spans[0, 0]) | (row >= spans[0, 1])) & (block >= 0)
    line = lax.broadcasted_iota(jnp.int32, (LANES, LANES), 0)

    def picker(head, of):
        return jnp.where((line == head) | (line == head + of), 1.0, 0.0).astype(jnp.bfloat16)

    own = refs[0]
    for part in range(parts):
        a, b = refs[1 + 2 * part : 3 + 2 * part]
        totals = jnp.concatenate([own[:, out.shape[1] :], a[:, width:], b[:, width:]], axis=1)
        for head in range(heads):
            pick = picker(head, heads)
            pick = jnp.concatenate([picker(part * heads + head, parts * heads), pick, pick], axis=0)
            total = jnp.dot(totals, pick, preferred_element_type=jnp.float32)
            total = jnp.where(total > 0, total, 1.0)
            cols = slice(head * HEAD_DIMENSION, (head + 1) * HEAD_DIMENSION)
            into = slice(part * width + cols.start, part * width + cols.stop)
            number = (
                own[:, into].astype(jnp.float32)
                + a[:, cols].astype(jnp.float32)
                + b[:, cols].astype(jnp.float32)
            )
            out[:, into] = jnp.where(keep, number / total, 0.0).astype(out.dtype)


SMEM = pl.BlockSpec(memory_space=pltpu.SMEM)
VMEM = pl.BlockSpec(memory_space=pltpu.VMEM)
HBM = pl.BlockSpec(memory_space=pltpu.HBM)


def in_hbm(array):
    return pltpu.with_memory_space_constraint(array, pltpu.HBM)


def work(queries, keys, values, dirty, spans):
    shards = lax.axis_size("seq")
    index = lax.axis_index("seq")
    rows, columns = keys.shape
    kv_heads = columns // HEAD_DIMENSION
    per = rows // BLOCK_ROWS
    back = WINDOW // rows
    reach = (back + 1) * SPAN
    swap = [(i, i ^ 1) for i in range(shards)]
    onward = [(i, i + 1) for i in range(1, shards - 1, 2)]

    parts = 2
    wide = queries.shape[1] // parts
    params = pltpu.CompilerParams(vmem_limit_bytes=VMEM_LIMIT)

    other = send(spans, swap)
    k_other = send(keys, swap)
    v_other = send(values, swap)
    *pieces, tail = pl.pallas_call(
        pack_kernel,
        out_shape=[
            jax.ShapeDtypeStruct((BLOCK_ROWS + (NOTE_ROWS if p == 0 else 0), wide), queries.dtype)
            for p in range(parts)
        ]
        + [jax.ShapeDtypeStruct((2 * reach + NOTE_ROWS, columns), keys.dtype)],
        in_specs=[SMEM] * 3 + [HBM] * 3,
        out_specs=[VMEM] * (parts + 1),
        scratch_shapes=[pltpu.SemaphoreType.DMA((parts + 2,))],
        compiler_params=params,
        cost_estimate=pl.CostEstimate(flops=1 << 20, bytes_accessed=4 << 20, transcendentals=0),
        name="pack",
    )(spans, other, dirty, in_hbm(keys), in_hbm(values), in_hbm(queries))
    near, far = [], []
    for piece in pieces:
        near.append(shift(piece, -back // 2))
        far.append(shift(piece, -back))
    tail = send(tail, onward)

    at = index.astype(jnp.int32).reshape(1)
    angles = jnp.asarray(row_angles())
    freq = jnp.asarray(lane_frequency()[None, :])
    part_heads = kv_heads // parts

    def payload(heads):
        return jax.ShapeDtypeStruct((BLOCK_ROWS, heads * HEAD_DIMENSION + LANES), jnp.bfloat16)

    by_head = pltpu.VMEM((kv_heads, 2 * rows, HEAD_DIMENSION), jnp.bfloat16)
    kr, vz, lv = pl.pallas_call(
        prepare_kernel,
        out_shape=(by_head, by_head, pltpu.VMEM((2 * rows, LANES), jnp.bfloat16)),
        in_specs=[SMEM] * 3 + [VMEM] * 2 + [HBM] * 4,
        out_specs=[VMEM] * 3,
        scratch_shapes=[
            pltpu.VMEM((2 * rows, columns), keys.dtype),
            pltpu.VMEM((2 * rows, columns), keys.dtype),
            pltpu.VMEM((2, -(-4 * per // 8) * 8, LANES), jnp.float32),
            pltpu.SemaphoreType.DMA((2, 2 * per)),
        ],
        compiler_params=params,
        cost_estimate=pl.CostEstimate(flops=1 << 24, bytes_accessed=20 << 20, transcendentals=0),
        name="prepare",
    )(at, spans, other, angles, freq, *map(in_hbm, (keys, k_other, values, v_other)))

    def visitor(kind, step, part, notes, query):
        count = {"own": per, "middle": 2 * per, "window": per}[kind] * BLOCK_ROWS
        heads = kv_heads if part is None else part_heads
        work = BLOCK_ROWS * 2 * heads * count
        edges = {"own": 1, "middle": 1, "window": 2}[kind]
        extra = [*notes, tail] if kind == "window" else notes
        return pl.pallas_call(
            functools.partial(visit_kernel, kind, step, shards, rows),
            out_shape=payload(2 * heads),
            in_specs=[SMEM] * 5 + [VMEM] * (6 + len(extra)),
            out_specs=VMEM,
            scratch_shapes=[
                pltpu.VMEM((BLOCK_ROWS, LANES), jnp.float32),
                pltpu.VMEM((2 * heads, BLOCK_ROWS, HEAD_DIMENSION), jnp.bfloat16),
                pltpu.VMEM((2 * heads, BLOCK_ROWS, HEAD_DIMENSION + LANES), jnp.float32),
                pltpu.VMEM((edges, heads, BLOCK_ROWS, HEAD_DIMENSION), jnp.bfloat16),
                pltpu.VMEM((edges, heads, BLOCK_ROWS, HEAD_DIMENSION), jnp.bfloat16),
                pltpu.VMEM((edges, BLOCK_ROWS, LANES), jnp.bfloat16),
            ],
            compiler_params=params,
            cost_estimate=pl.CostEstimate(
                flops=work * 4 * HEAD_DIMENSION, bytes_accessed=6 << 20, transcendentals=2 * work
            ),
        )(
            at, jnp.full((1,), part or 0, jnp.int32), spans, other, dirty,
            *extra, angles, freq, kr, vz, lv, query,
        )

    middle, window = [], []
    for p in range(parts):
        got = visitor("middle", back // 2, p, [near[0]], near[p])
        middle.append(shift(got, back // 2))
        got = visitor("window", back, p, [near[0], far[0]], far[p])
        window.append(shift(got, back))
    own = visitor("own", 0, None, [], queries)
    sums = [own] + [x for p in range(parts) for x in (middle[p], window[p])]
    return pl.pallas_call(
        functools.partial(last_kernel, rows, parts),
        out_shape=jax.ShapeDtypeStruct(queries.shape, queries.dtype),
        in_specs=[SMEM] * 3 + [VMEM] * len(sums),
        out_specs=VMEM,
        compiler_params=params,
        name="last",
    )(spans, dirty, at, *sums)


def solution(mesh):
    placed = (
        P(("groups", "seq"), None),
        P(("groups", "seq"), None),
        P(("groups", "seq"), None),
        P(("groups", "seq")),
        P(("groups", "seq"), None),
    )
    return jax.shard_map(
        work, mesh=mesh, in_specs=placed, out_specs=P(("groups", "seq"), None), check_vma=False
    )
```

```python
import functools
import math

import jax
import jax.numpy as jnp
import numpy as np
from jax import lax
from jax.experimental import pallas as pl
from jax.experimental.pallas import tpu as pltpu
from jax.sharding import PartitionSpec as P


HEAD_DIMENSION = 128
WINDOW = 4096
BLOCK_ROWS = 256
SPAN = 32

SOFTCAP = 50.0
QUERY_SCALE = 144.0 ** (-0.5)
TO_TANH = 1.0 / SOFTCAP
TO_EXP2 = SOFTCAP * math.log2(math.e)

HALF = HEAD_DIMENSION // 2
LANES = 128
NOTE_ROWS = 8
SECOND_PART = 3
DIGIT = 32
VMEM_LIMIT = 32 << 20


def lane_frequency():
    order = np.arange(HEAD_DIMENSION) % HALF
    return np.exp(order * (-2.0 * math.log(10000.0) / HEAD_DIMENSION)).astype(np.float32)


def row_angles():
    angle = np.arange(BLOCK_ROWS, dtype=np.float64)[:, None] * lane_frequency().astype(np.float64)[None, :]
    sign = np.where(np.arange(HEAD_DIMENSION) < HALF, -1.0, 1.0)[None, :]
    return np.stack([np.cos(angle), np.sin(angle) * sign]).astype(np.float32)


def send(array, pairs):
    return lax.ppermute(array, "seq", pairs)


def shift(array, by):
    count = lax.axis_size("seq")
    return send(array, [(i, i + by) for i in range(count) if 0 <= i + by < count])


class Frame:
    def __init__(self, spans, rows):
        self.spans, self.rows = spans, rows

    def tile(self, shard_step, row):
        start, length = self.spans[shard_step]
        first = shard_step * self.rows + row
        for step in range(min(shard_step, 0), max(shard_step, 0)):
            _, other = self.spans[step]
            first = first - other if step >= 0 else first + other
        first = first - jnp.clip(row - start, 0, length)
        begin = start - row
        end = begin + length
        gone = jnp.clip(end, 0, BLOCK_ROWS) - jnp.clip(begin, 0, BLOCK_ROWS)
        return first, first - gone, begin, end


def by_parity(odd, mine, other):
    mine = [jnp.where(odd == 1, b, a) for a, b in zip(mine, other)], [
        jnp.where(odd == 1, a, b) for a, b in zip(mine, other)
    ]
    return mine


def write_note(ref, numbers):
    shape = (NOTE_ROWS, ref.shape[1])
    lane = lax.broadcasted_iota(jnp.int32, shape, 1)
    row = jnp.zeros(shape, jnp.int32)
    for k, number in enumerate(numbers):
        row = jnp.where(lane == 2 * k, number // DIGIT, jnp.where(lane == 2 * k + 1, number % DIGIT, row))
    ref[ref.shape[0] - NOTE_ROWS :, :] = row.astype(jnp.float32).astype(jnp.bfloat16)


def read_note(note, count):
    low = note.astype(jnp.float32)
    shape = (NOTE_ROWS, LANES)
    lane = lax.broadcasted_iota(jnp.int32, shape, 1)
    first = lax.broadcasted_iota(jnp.int32, shape, 0) == 0
    out = []
    for k in range(count):
        digits = jnp.where(lane == 2 * k, low * DIGIT, jnp.where(lane == 2 * k + 1, low, 0.0))
        out.append(jnp.sum(jnp.where(first, digits, 0.0)).astype(jnp.int32))
    return out


def wave(offsets, freq):
    count = -(-len(offsets) // 8) * 8
    row = lax.broadcasted_iota(jnp.int32, (count, LANES), 0)
    lane = lax.broadcasted_iota(jnp.int32, (count, LANES), 1)
    value = jnp.zeros((count, LANES), jnp.int32)
    for k, offset in enumerate(offsets):
        value = jnp.where(row == k, offset, value)
    angle = value.astype(jnp.float32) * freq
    sine = jnp.sin(angle)
    return jnp.cos(angle), jnp.where(lane < HALF, -sine, sine)


def rope_tables(angles, begin, waves, at, scale):
    cosine, sine = waves
    row = lax.broadcasted_iota(jnp.int32, (BLOCK_ROWS, LANES), 0)
    early = row < begin
    c = jnp.where(early, cosine[at : at + 1], cosine[at + 1 : at + 2])
    s = jnp.where(early, sine[at : at + 1], sine[at + 1 : at + 2])
    rc, rs = angles[0], angles[1]
    return (rc * c - rs * s) * scale, (rs * c + rc * s) * scale


def rotate(x, c, s):
    x = x.astype(jnp.float32)
    return (x * c + pltpu.roll(x, HALF, 1) * s).astype(jnp.bfloat16)


def places(tile, dim, shape):
    first, later, begin, _ = tile
    row = lax.broadcasted_iota(jnp.int32, shape, dim)
    return row + jnp.where(row < begin, first, later)


def visit(kind, index, block, frame, freq, angles, low, query, keys, edge, out, scratch):
    kr, vz, lv = keys
    rot, acc, ke, ve, le = scratch
    odd = lax.rem(index, 2)
    per = frame.rows // BLOCK_ROWS
    q_heads = acc.shape[0]
    kv_heads = q_heads // 2
    pair = [frame.tile(s, block * BLOCK_ROWS) for s in edge["block"]]
    tile = [jnp.where(odd == 1, b, a) for a, b in zip(*pair)]
    waves = wave([tile[0], tile[1]], freq)
    c, s = rope_tables(angles, tile[2], waves, 0, QUERY_SCALE)
    for head in range(q_heads):
        cols = slice(head * HEAD_DIMENSION, (head + 1) * HEAD_DIMENSION)
        rot[head] = rotate(query(cols), c, s)
    own = places(tile, 0, (BLOCK_ROWS, 1))

    def add(head, keys_of, values_of, keep, fresh):
        score = lax.dot_general(
            rot[head], keys_of, (((1,), (1,)), ((), ())), preferred_element_type=jnp.float32
        )
        weight = jnp.exp2(jnp.tanh(score * TO_TANH) * TO_EXP2)
        if keep is not None:
            weight = jnp.where(keep, weight, 0.0)
        both = jnp.dot(weight.astype(jnp.bfloat16), values_of, preferred_element_type=jnp.float32)
        acc[head] = both if fresh else acc[head] + both

    def many(begin, count, fresh):
        some = pl.ds(pl.multiple_of(begin * BLOCK_ROWS, BLOCK_ROWS), count * BLOCK_ROWS)

        def one(i, carry):
            v = jnp.concatenate([vz[low + i, some, :], lv[some, :]], axis=1)
            for g in range(2):
                add(2 * i + g, kr[low + i, some, :], v, None, fresh)
            return carry

        lax.fori_loop(0, kv_heads, one, 0)

    def single(at, carry):
        some = pl.ds(pl.multiple_of(at * BLOCK_ROWS, BLOCK_ROWS), BLOCK_ROWS)
        live = lv[some, :]
        for i in range(kv_heads):
            v = jnp.concatenate([vz[low + i, some, :], live], axis=1)
            for g in range(2):
                add(2 * i + g, kr[low + i, some, :], v, None, False)
        return carry

    def stage(slot, at):
        some = pl.ds(pl.multiple_of(at * BLOCK_ROWS, BLOCK_ROWS), BLOCK_ROWS)
        for i in range(kv_heads):
            ke[slot, i] = kr[low + i, some, :]
            ve[slot, i] = vz[low + i, some, :]
        le[slot] = lv[some, :]

    def masked(slot, keep, fresh):
        for i in range(kv_heads):
            v = jnp.concatenate([ve[slot, i], le[slot]], axis=1)
            for g in range(2):
                add(2 * i + g, ke[slot, i], v, keep, fresh)

    def places_at(at):
        pair = [frame.tile(s, at * BLOCK_ROWS) for s in (0, 1)]
        tile = [jnp.where(odd == 1, b, a) for a, b in zip(*pair)]
        return places(tile, 1, (1, BLOCK_ROWS))

    if kind == "middle":
        many(0, 2 * per, True)
    elif kind == "own":
        stage(0, odd * per + block)
        masked(0, own >= places_at(block), True)

        @pl.when(odd == 1)
        def _():
            many(0, per, False)

        lax.fori_loop(odd * per, odd * per + block, single, 0)
    else:
        first = odd * per + block
        tail_k, tail_v, tail_tile = edge["tail"]

        @pl.when(first > 0)
        def _():
            stage(0, first - 1)

        @pl.when(first == 0)
        def _():
            reach = tail_k.shape[0]
            row = lax.broadcasted_iota(jnp.int32, (BLOCK_ROWS, LANES), 0)
            live = (row < tail_tile[2]) | (row >= tail_tile[3])
            live = live & (row >= BLOCK_ROWS - reach) & (index > 0)
            c, s = rope_tables(angles, tail_tile[2], wave(list(tail_tile[:2]), freq), 0, 1.0)
            le[0] = jnp.where(live, 1.0, 0.0).astype(jnp.bfloat16)
            zero = jnp.zeros((BLOCK_ROWS - reach, HEAD_DIMENSION), jnp.bfloat16)
            for i in range(kv_heads):
                cols = slice((low + i) * HEAD_DIMENSION, (low + i + 1) * HEAD_DIMENSION)
                ke[0, i] = rotate(jnp.concatenate([zero, tail_k[:, cols]], axis=0), c, s)
                ve[0, i] = jnp.concatenate([zero, tail_v[:, cols]], axis=0) * le[0]

        stage(1, first)
        before = places_at(block - 1)
        before = jnp.where(first == 0, places(tail_tile, 1, (1, BLOCK_ROWS)), before)
        masked(0, own - before < WINDOW, True)
        masked(1, own - places_at(block) < WINDOW, False)

        @pl.when(odd == 0)
        def _():
            many(per, per, False)

        lax.fori_loop(first + 1, (odd + 1) * per, single, 0)

    lane = lax.broadcasted_iota(jnp.int32, (BLOCK_ROWS, LANES), 1)
    sums = jnp.zeros((BLOCK_ROWS, LANES), jnp.float32)
    for head in range(q_heads):
        cols = slice(head * HEAD_DIMENSION, (head + 1) * HEAD_DIMENSION)
        out[:BLOCK_ROWS, cols] = acc[head, :, :HEAD_DIMENSION].astype(jnp.bfloat16)
        t = acc[head, :, HEAD_DIMENSION:]
        high = t.astype(jnp.bfloat16).astype(jnp.float32)
        sums = jnp.where(lane == head, high, jnp.where(lane == head + q_heads, t - high, sums))
    sums = jnp.transpose(sums).astype(jnp.bfloat16)
    groups = [sums[k * NOTE_ROWS : (k + 1) * NOTE_ROWS] for k in range(-(-2 * q_heads // NOTE_ROWS))]
    rest = out.shape[1] - len(groups) * BLOCK_ROWS
    out[BLOCK_ROWS:, :] = jnp.concatenate(groups + [jnp.zeros((NOTE_ROWS, rest), jnp.bfloat16)], axis=1)


def cut_kernel(query, piece, sem):
    copy = pltpu.make_async_copy(query.at[:, : piece.shape[1]], piece, sem)
    copy.start()
    copy.wait()


def pack_kernel(spans, other, dirty, keys, values, query, piece, tail, note, sem):
    rows = keys.shape[0]
    reach = (tail.shape[0] - NOTE_ROWS) // 2
    copies = [
        (query.at[:, query.shape[1] - piece.shape[1] :], piece),
        (keys.at[rows - reach :], tail.at[:reach]),
        (values.at[rows - reach :], tail.at[reach : 2 * reach]),
    ]
    copies = [pltpu.make_async_copy(a, b, sem.at[k]) for k, (a, b) in enumerate(copies)]
    for copy in copies:
        copy.start()
    mine = [lax.rem(spans[0, 0], rows), spans[0, 1] - spans[0, 0]]
    write_note(tail, mine)
    others = [lax.rem(other[0, 0], rows), other[0, 1] - other[0, 0]]
    for k, number in enumerate(mine + others + [dirty[0] + 1]):
        note[k] = number
    for k in range(5, note.shape[0]):
        note[k] = 0
    for copy in copies:
        copy.wait()


def chip_spans(index, rows, spans, other):
    mine = [lax.rem(spans[0, 0], rows), spans[0, 1] - spans[0, 0]]
    others = [lax.rem(other[0, 0], rows), other[0, 1] - other[0, 0]]
    return by_parity(lax.rem(index, 2), mine, others)


def prepare_kernel(
    index_ref, spans, other, angles, freq, k_own, k_other, v_own, v_other, kr, vz, lv, kb, vb, waves, sem,
):
    rows = k_own.shape[0]
    per = rows // BLOCK_ROWS
    kv_heads = kr.shape[0]
    index = index_ref[0]
    odd = lax.rem(index, 2)

    def copies(i, pair):
        into = pl.ds(pl.multiple_of(i * BLOCK_ROWS, BLOCK_ROWS), BLOCK_ROWS)
        t = lax.rem(i, per)
        of = pl.ds(pl.multiple_of(t * BLOCK_ROWS, BLOCK_ROWS), BLOCK_ROWS)
        return [
            pltpu.make_async_copy(ref.at[of, :], buf.at[into, :], sem.at[k, i])
            for k, (ref, buf) in enumerate(zip(pair, (kb, vb)))
        ]

    for i in range(2 * per):
        for copy in copies(i, (k_own, v_own) if i < per else (k_other, v_other)):
            copy.start()
    frame = Frame(dict(enumerate(chip_spans(index, rows, spans, other))), rows)
    tiles = [frame.tile(s, t * BLOCK_ROWS) for s in (0, 1) for t in range(per)]
    waves[0], waves[1] = wave([o for tile in tiles for o in tile[:2]], freq[...])
    row = lax.broadcasted_iota(jnp.int32, (BLOCK_ROWS, LANES), 0)

    def one(i, carry):
        for copy in copies(i, (k_own, v_own)):
            copy.wait()
        shard = jnp.where(i < per, odd, 1 - odd)
        t = lax.rem(i, per)
        at = shard * per + t
        tile = [
            jnp.where(shard == 1, b, a)
            for a, b in zip(*[frame.tile(s, t * BLOCK_ROWS) for s in (0, 1)])
        ]
        rows_of = (waves[0, pl.ds(2 * at, 2), :], waves[1, pl.ds(2 * at, 2), :])
        c, s = rope_tables(angles, tile[2], rows_of, 0, 1.0)
        live = jnp.where((row < tile[2]) | (row >= tile[3]), 1.0, 0.0).astype(jnp.bfloat16)
        into = pl.ds(pl.multiple_of(at * BLOCK_ROWS, BLOCK_ROWS), BLOCK_ROWS)
        of = pl.ds(pl.multiple_of(i * BLOCK_ROWS, BLOCK_ROWS), BLOCK_ROWS)
        lv[into, :] = live
        for h in range(kv_heads):
            cols = slice(h * HEAD_DIMENSION, (h + 1) * HEAD_DIMENSION)
            kr[h, into, :] = rotate(kb[of, cols], c, s)
            vz[h, into, :] = vb[of, cols] * live
        return carry

    lax.fori_loop(0, 2 * per, one, 0)


def visit_kernel(kind, step, shards, rows, low, index_ref, spans, other, dirty, *refs):
    index = index_ref[0]
    odd = lax.rem(index, 2)
    held = dict(enumerate(chip_spans(index, rows, spans, other)))
    block = dirty[0]
    through = lax.rem(index // 2, 2) == 1
    if kind == "window":
        near_note, note, tail, *refs = refs
        held[2] = (0, near_note[1] + near_note[3])
        held[3] = (0, 0)
    elif kind == "middle":
        note, direct, relayed, *refs = refs
    if kind != "own":
        held[step], held[step + 1] = by_parity(odd, (note[0], note[1]), (note[2], note[3]))
        block = note[4] - 1
    angles, freq, kr, vz, lv, *refs = refs
    if kind == "middle":

        def query(cols):
            a = direct[:BLOCK_ROWS, cols].astype(jnp.float32)
            return jnp.where(through, relayed[:BLOCK_ROWS, cols].astype(jnp.float32), a)
    else:
        queries, *refs = refs
        query = lambda cols: queries[:BLOCK_ROWS, cols]
    out, *scratch = refs
    valid = (index + step < shards) & (block >= 0)

    @pl.when(jnp.logical_not(valid))
    def _():
        out[...] = jnp.zeros(out.shape, out.dtype)

    @pl.when(valid)
    def _():
        edge = {"block": (step, step + 1)}
        if kind == "window":
            held[-1] = read_note(tail[tail.shape[0] - NOTE_ROWS :, :LANES], 2)
            reach = (tail.shape[0] - NOTE_ROWS) // 2
            tail_tile = Frame(held, rows).tile(-1, rows - BLOCK_ROWS)
            edge["tail"] = tail.at[:reach, :], tail.at[reach : 2 * reach, :], tail_tile
        frame = Frame(held, rows)
        keys = (kr, vz, lv)
        visit(kind, index, block, frame, freq[...], angles, low, query, keys, edge, out, scratch)


def last_kernel(rows, low, spans, dirty, index_ref, own, a, b, *refs):
    out, result, sem = refs[-3:]
    index = index_ref[0]
    heads = result.shape[1] // HEAD_DIMENSION
    block = dirty[0]
    first = index * rows + jnp.maximum(block, 0) * BLOCK_ROWS
    row = lax.broadcasted_iota(jnp.int32, (BLOCK_ROWS, LANES), 0) + first
    keep = ((row < spans[0, 0]) | (row >= spans[0, 1])) & (block >= 0)
    rows_of, heads_of = [], []
    for ref, count, lowest in ((own, own.shape[1] // HEAD_DIMENSION, 0), (a, heads, low), (b, heads, low)):
        for k in range(-(-2 * count // NOTE_ROWS)):
            rows_of.append(ref[BLOCK_ROWS:, k * BLOCK_ROWS : (k + 1) * BLOCK_ROWS].astype(jnp.float32))
            for r in range(k * NOTE_ROWS, (k + 1) * NOTE_ROWS):
                heads_of.append(lowest + r % count if r < 2 * count else -1)
    rows_of.append(jnp.zeros((LANES - len(heads_of), BLOCK_ROWS), jnp.float32))
    totals = jnp.transpose(jnp.concatenate(rows_of, axis=0)).astype(jnp.bfloat16)
    line = lax.broadcasted_iota(jnp.int32, (LANES, LANES), 0)
    for head in range(heads):
        hit = [line == r for r, h in enumerate(heads_of) if h == low + head]
        pick = jnp.where(functools.reduce(jnp.logical_or, hit), 1.0, 0.0).astype(jnp.bfloat16)
        total = jnp.dot(totals, pick, preferred_element_type=jnp.float32)
        total = jnp.where(total > 0, total, 1.0)
        cols = slice(head * HEAD_DIMENSION, (head + 1) * HEAD_DIMENSION)
        from_own = slice(cols.start + low * HEAD_DIMENSION, cols.stop + low * HEAD_DIMENSION)
        number = (
            own[:BLOCK_ROWS, from_own].astype(jnp.float32)
            + a[:BLOCK_ROWS, cols].astype(jnp.float32)
            + b[:BLOCK_ROWS, cols].astype(jnp.float32)
        )
        result[:, cols] = jnp.where(keep, number / total, 0.0).astype(result.dtype)
    copy = pltpu.make_async_copy(
        result, out.at[:, low * HEAD_DIMENSION : (low + heads) * HEAD_DIMENSION], sem
    )
    copy.start()
    copy.wait()


SMEM = pl.BlockSpec(memory_space=pltpu.SMEM)
VMEM = pl.BlockSpec(memory_space=pltpu.VMEM)
HBM = pl.BlockSpec(memory_space=pltpu.HBM)


def in_hbm(array):
    return pltpu.with_memory_space_constraint(array, pltpu.HBM)


def work(queries, keys, values, dirty, spans):
    shards = lax.axis_size("seq")
    index = lax.axis_index("seq")
    rows, columns = keys.shape
    kv_heads = columns // HEAD_DIMENSION
    per = rows // BLOCK_ROWS
    back = WINDOW // rows
    reach = (back + 1) * SPAN
    swap = [(i, i ^ 1) for i in range(shards)]
    onward = [(i, i + 1) for i in range(1, shards - 1, 2)]

    second = kv_heads * SECOND_PART // 8
    parts = [(0, kv_heads - second), (kv_heads - second, second)]
    params = pltpu.CompilerParams(vmem_limit_bytes=VMEM_LIMIT)

    other = send(spans, swap)
    k_other = send(keys, swap)
    v_other = send(values, swap)
    widths = [2 * heads * HEAD_DIMENSION for _, heads in parts]
    piece = pl.pallas_call(
        cut_kernel,
        out_shape=jax.ShapeDtypeStruct((BLOCK_ROWS, widths[0]), queries.dtype),
        in_specs=[HBM],
        out_specs=VMEM,
        scratch_shapes=[pltpu.SemaphoreType.DMA(())],
        compiler_params=params,
        cost_estimate=pl.CostEstimate(flops=1, bytes_accessed=1 << 20, transcendentals=0),
        name="cut",
    )(in_hbm(queries))
    rest, tail, note = pl.pallas_call(
        pack_kernel,
        out_shape=[
            jax.ShapeDtypeStruct((BLOCK_ROWS, widths[1]), queries.dtype),
            jax.ShapeDtypeStruct((2 * reach + NOTE_ROWS, columns), keys.dtype),
            jax.ShapeDtypeStruct((8,), jnp.int32),
        ],
        in_specs=[SMEM] * 3 + [HBM] * 3,
        out_specs=[VMEM] * 2 + [SMEM],
        scratch_shapes=[pltpu.SemaphoreType.DMA((3,))],
        compiler_params=params,
        cost_estimate=pl.CostEstimate(flops=1, bytes_accessed=2 << 20, transcendentals=0),
        name="pack",
    )(spans, other, dirty, in_hbm(keys), in_hbm(values), in_hbm(queries))
    pieces = [piece, rest]
    odd_to_even = [(i, i - back // 2) for i in range(shards) if i // 2 % 2 == 1]
    even_to_odd = [(i, i + back // 2) for i in range(shards - back // 2) if i // 2 % 2 == 0]
    far = [shift(piece, -back) for piece in pieces]
    near = [send(piece, odd_to_even) for piece in pieces]
    relay = [send(piece, even_to_odd) for piece in far]
    tail = send(tail, onward)
    near_note = shift(note, -back // 2)
    far_note = shift(note, -back)

    at = index.astype(jnp.int32).reshape(1)
    angles = jnp.asarray(row_angles())
    freq = jnp.asarray(lane_frequency()[None, :])

    def payload(heads):
        return jax.ShapeDtypeStruct((BLOCK_ROWS + NOTE_ROWS, heads * HEAD_DIMENSION), jnp.bfloat16)

    by_head = pltpu.VMEM((kv_heads, 2 * rows, HEAD_DIMENSION), jnp.bfloat16)
    kr, vz, lv = pl.pallas_call(
        prepare_kernel,
        out_shape=(by_head, by_head, pltpu.VMEM((2 * rows, LANES), jnp.bfloat16)),
        in_specs=[SMEM] * 3 + [VMEM] * 2 + [HBM] * 4,
        out_specs=[VMEM] * 3,
        scratch_shapes=[
            pltpu.VMEM((2 * rows, columns), keys.dtype),
            pltpu.VMEM((2 * rows, columns), keys.dtype),
            pltpu.VMEM((2, -(-4 * per // 8) * 8, LANES), jnp.float32),
            pltpu.SemaphoreType.DMA((2, 2 * per)),
        ],
        compiler_params=params,
        cost_estimate=pl.CostEstimate(flops=1 << 24, bytes_accessed=20 << 20, transcendentals=0),
        name="prepare",
    )(at, spans, other, angles, freq, *map(in_hbm, (keys, k_other, values, v_other)))

    def visitor(kind, step, part, small, notes, query):
        low, heads = (0, kv_heads) if part is None else parts[part]
        count = {"own": per, "middle": 2 * per, "window": per}[kind] * BLOCK_ROWS
        work = BLOCK_ROWS * 2 * heads * count
        edges = {"own": 1, "middle": 1, "window": 2}[kind]
        return pl.pallas_call(
            functools.partial(visit_kernel, kind, step, shards, rows, low),
            out_shape=payload(2 * heads),
            in_specs=[SMEM] * (4 + len(small)) + [VMEM] * (5 + len(notes) + len(query)),
            out_specs=VMEM,
            scratch_shapes=[
                pltpu.VMEM((2 * heads, BLOCK_ROWS, HEAD_DIMENSION), jnp.bfloat16),
                pltpu.VMEM((2 * heads, BLOCK_ROWS, HEAD_DIMENSION + LANES), jnp.float32),
                pltpu.VMEM((edges, heads, BLOCK_ROWS, HEAD_DIMENSION), jnp.bfloat16),
                pltpu.VMEM((edges, heads, BLOCK_ROWS, HEAD_DIMENSION), jnp.bfloat16),
                pltpu.VMEM((edges, BLOCK_ROWS, LANES), jnp.bfloat16),
            ],
            compiler_params=params,
            cost_estimate=pl.CostEstimate(
                flops=work * 4 * HEAD_DIMENSION, bytes_accessed=6 << 20, transcendentals=2 * work
            ),
        )(at, spans, other, dirty, *small, *notes, angles, freq, kr, vz, lv, *query)

    middle, window = [], []
    for p in range(len(parts)):
        got = visitor("window", back, p, [near_note, far_note], [tail], [far[p]])
        window.append(shift(got, back))
        got = visitor("middle", back // 2, p, [near_note], [near[p], relay[p]], [])
        middle.append(shift(got, back // 2))
    own = visitor("own", 0, None, [], [], [queries])
    result = []
    for (low, heads), a, b in zip(parts, middle, window):
        result = [
            pl.pallas_call(
                functools.partial(last_kernel, rows, 2 * low),
                out_shape=jax.ShapeDtypeStruct(queries.shape, queries.dtype),
                in_specs=[SMEM] * 3 + [VMEM] * 3 + [HBM] * len(result),
                out_specs=HBM,
                scratch_shapes=[
                    pltpu.VMEM((BLOCK_ROWS, 2 * heads * HEAD_DIMENSION), queries.dtype),
                    pltpu.SemaphoreType.DMA(()),
                ],
                input_output_aliases={6: 0} if result else {},
                compiler_params=params,
                name="last",
            )(spans, dirty, at, own, a, b, *result)
        ]
    return result[0]


def solution(mesh):
    placed = (
        P(("groups", "seq"), None),
        P(("groups", "seq"), None),
        P(("groups", "seq"), None),
        P(("groups", "seq")),
        P(("groups", "seq"), None),
    )
    return jax.shard_map(
        work, mesh=mesh, in_specs=placed, out_specs=P(("groups", "seq"), None), check_vma=False
    )
```

```python
import functools
import math

import jax
import jax.numpy as jnp
import numpy as np
from jax import lax
from jax.experimental import pallas as pl
from jax.experimental.pallas import tpu as pltpu
from jax.sharding import PartitionSpec as P


HEAD_DIMENSION = 128
WINDOW = 4096
BLOCK_ROWS = 256
SPAN = 32

SOFTCAP = 50.0
QUERY_SCALE = 144.0 ** (-0.5)
TO_TANH = 1.0 / SOFTCAP
TO_EXP2 = SOFTCAP * math.log2(math.e)

HALF = HEAD_DIMENSION // 2
LANES = 128
NOTE_ROWS = 8
SECOND_PART = 3
DIGIT = 32
VMEM_LIMIT = 32 << 20


def lane_frequency():
    order = np.arange(HEAD_DIMENSION) % HALF
    return np.exp(order * (-2.0 * math.log(10000.0) / HEAD_DIMENSION)).astype(np.float32)


def row_angles():
    angle = np.arange(BLOCK_ROWS, dtype=np.float64)[:, None] * lane_frequency().astype(np.float64)[None, :]
    sign = np.where(np.arange(HEAD_DIMENSION) < HALF, -1.0, 1.0)[None, :]
    return np.stack([np.cos(angle), np.sin(angle) * sign]).astype(np.float32)


def send(array, pairs):
    return lax.ppermute(array, "seq", pairs)


def shift(array, by):
    count = lax.axis_size("seq")
    return send(array, [(i, i + by) for i in range(count) if 0 <= i + by < count])


class Frame:
    def __init__(self, spans, rows):
        self.spans, self.rows = spans, rows

    def tile(self, shard_step, row):
        start, length = self.spans[shard_step]
        first = shard_step * self.rows + row
        for step in range(min(shard_step, 0), max(shard_step, 0)):
            _, other = self.spans[step]
            first = first - other if step >= 0 else first + other
        first = first - jnp.clip(row - start, 0, length)
        begin = start - row
        end = begin + length
        gone = jnp.clip(end, 0, BLOCK_ROWS) - jnp.clip(begin, 0, BLOCK_ROWS)
        return first, first - gone, begin, end


def by_parity(odd, mine, other):
    mine = [jnp.where(odd == 1, b, a) for a, b in zip(mine, other)], [
        jnp.where(odd == 1, a, b) for a, b in zip(mine, other)
    ]
    return mine


def write_note(ref, numbers):
    shape = (NOTE_ROWS, ref.shape[1])
    lane = lax.broadcasted_iota(jnp.int32, shape, 1)
    row = jnp.zeros(shape, jnp.int32)
    for k, number in enumerate(numbers):
        row = jnp.where(lane == 2 * k, number // DIGIT, jnp.where(lane == 2 * k + 1, number % DIGIT, row))
    ref[ref.shape[0] - NOTE_ROWS :, :] = row.astype(jnp.float32).astype(jnp.bfloat16)


def read_note(note, count):
    low = note.astype(jnp.float32)
    shape = (NOTE_ROWS, LANES)
    lane = lax.broadcasted_iota(jnp.int32, shape, 1)
    first = lax.broadcasted_iota(jnp.int32, shape, 0) == 0
    out = []
    for k in range(count):
        digits = jnp.where(lane == 2 * k, low * DIGIT, jnp.where(lane == 2 * k + 1, low, 0.0))
        out.append(jnp.sum(jnp.where(first, digits, 0.0)).astype(jnp.int32))
    return out


def wave(offsets, freq):
    count = -(-len(offsets) // 8) * 8
    row = lax.broadcasted_iota(jnp.int32, (count, LANES), 0)
    lane = lax.broadcasted_iota(jnp.int32, (count, LANES), 1)
    value = jnp.zeros((count, LANES), jnp.int32)
    for k, offset in enumerate(offsets):
        value = jnp.where(row == k, offset, value)
    angle = value.astype(jnp.float32) * freq
    sine = jnp.sin(angle)
    return jnp.cos(angle), jnp.where(lane < HALF, -sine, sine)


def rope_tables(angles, begin, waves, at, scale):
    cosine, sine = waves
    row = lax.broadcasted_iota(jnp.int32, (BLOCK_ROWS, LANES), 0)
    early = row < begin
    c = jnp.where(early, cosine[at : at + 1], cosine[at + 1 : at + 2])
    s = jnp.where(early, sine[at : at + 1], sine[at + 1 : at + 2])
    rc, rs = angles[0], angles[1]
    return (rc * c - rs * s) * scale, (rs * c + rc * s) * scale


def rotate(x, c, s):
    x = x.astype(jnp.float32)
    return (x * c + pltpu.roll(x, HALF, 1) * s).astype(jnp.bfloat16)


def places(tile, dim, shape):
    first, later, begin, _ = tile
    row = lax.broadcasted_iota(jnp.int32, shape, dim)
    return row + jnp.where(row < begin, first, later)


def visit(kind, index, block, frame, freq, angles, low, query, keys, edge, out, scratch):
    kr, vz, lv = keys
    rot, acc, ke, ve, le = scratch
    odd = lax.rem(index, 2)
    per = frame.rows // BLOCK_ROWS
    q_heads = acc.shape[0]
    kv_heads = q_heads // 2
    pair = [frame.tile(s, block * BLOCK_ROWS) for s in edge["block"]]
    tile = [jnp.where(odd == 1, b, a) for a, b in zip(*pair)]
    waves = wave([tile[0], tile[1]], freq)
    c, s = rope_tables(angles, tile[2], waves, 0, QUERY_SCALE)
    for head in range(q_heads):
        cols = slice(head * HEAD_DIMENSION, (head + 1) * HEAD_DIMENSION)
        rot[head] = rotate(query(cols), c, s)
    own = places(tile, 0, (BLOCK_ROWS, 1))

    def add(head, keys_of, values_of, keep, fresh):
        score = lax.dot_general(
            rot[head], keys_of, (((1,), (1,)), ((), ())), preferred_element_type=jnp.float32
        )
        weight = jnp.exp2(jnp.tanh(score * TO_TANH) * TO_EXP2)
        if keep is not None:
            weight = jnp.where(keep, weight, 0.0)
        both = jnp.dot(weight.astype(jnp.bfloat16), values_of, preferred_element_type=jnp.float32)
        acc[head] = both if fresh else acc[head] + both

    def many(begin, count, fresh):
        some = pl.ds(pl.multiple_of(begin * BLOCK_ROWS, BLOCK_ROWS), count * BLOCK_ROWS)

        def one(i, carry):
            v = jnp.concatenate([vz[low + i, some, :], lv[some, :]], axis=1)
            for g in range(2):
                add(2 * i + g, kr[low + i, some, :], v, None, fresh)
            return carry

        lax.fori_loop(0, kv_heads, one, 0)

    def single(at, carry):
        some = pl.ds(pl.multiple_of(at * BLOCK_ROWS, BLOCK_ROWS), BLOCK_ROWS)
        live = lv[some, :]
        for i in range(kv_heads):
            v = jnp.concatenate([vz[low + i, some, :], live], axis=1)
            for g in range(2):
                add(2 * i + g, kr[low + i, some, :], v, None, False)
        return carry

    def stage(slot, at):
        some = pl.ds(pl.multiple_of(at * BLOCK_ROWS, BLOCK_ROWS), BLOCK_ROWS)
        for i in range(kv_heads):
            ke[slot, i] = kr[low + i, some, :]
            ve[slot, i] = vz[low + i, some, :]
        le[slot] = lv[some, :]

    def masked(slot, keep, fresh):
        for i in range(kv_heads):
            v = jnp.concatenate([ve[slot, i], le[slot]], axis=1)
            for g in range(2):
                add(2 * i + g, ke[slot, i], v, keep, fresh)

    def places_at(at):
        pair = [frame.tile(s, at * BLOCK_ROWS) for s in (0, 1)]
        tile = [jnp.where(odd == 1, b, a) for a, b in zip(*pair)]
        return places(tile, 1, (1, BLOCK_ROWS))

    if kind == "middle":
        many(0, 2 * per, True)
    elif kind == "own":
        stage(0, odd * per + block)
        masked(0, own >= places_at(block), True)

        @pl.when(odd == 1)
        def _():
            many(0, per, False)

        lax.fori_loop(odd * per, odd * per + block, single, 0)
    else:
        first = odd * per + block
        tail_k, tail_v, tail_tile = edge["tail"]

        @pl.when(first > 0)
        def _():
            stage(0, first - 1)

        @pl.when(first == 0)
        def _():
            reach = tail_k.shape[0]
            row = lax.broadcasted_iota(jnp.int32, (BLOCK_ROWS, LANES), 0)
            live = (row < tail_tile[2]) | (row >= tail_tile[3])
            live = live & (row >= BLOCK_ROWS - reach) & (index > 0)
            c, s = rope_tables(angles, tail_tile[2], wave(list(tail_tile[:2]), freq), 0, 1.0)
            le[0] = jnp.where(live, 1.0, 0.0).astype(jnp.bfloat16)
            zero = jnp.zeros((BLOCK_ROWS - reach, HEAD_DIMENSION), jnp.bfloat16)
            for i in range(kv_heads):
                cols = slice((low + i) * HEAD_DIMENSION, (low + i + 1) * HEAD_DIMENSION)
                ke[0, i] = rotate(jnp.concatenate([zero, tail_k[:, cols]], axis=0), c, s)
                ve[0, i] = jnp.concatenate([zero, tail_v[:, cols]], axis=0) * le[0]

        stage(1, first)
        inside = block > 0
        row = jnp.where(inside, block - 1, per - 1) * BLOCK_ROWS
        last = frame.tile(0, (per - 1) * BLOCK_ROWS)
        even = [jnp.where(inside, a, b) for a, b in zip(frame.tile(0, row), tail_tile)]
        other = [jnp.where(inside, a, b) for a, b in zip(frame.tile(1, row), last)]
        tile = [jnp.where(odd == 1, b, a) for a, b in zip(even, other)]
        before = places(tile, 1, (1, BLOCK_ROWS))
        masked(0, own - before < WINDOW, True)
        masked(1, own - places_at(block) < WINDOW, False)

        @pl.when(odd == 0)
        def _():
            many(per, per, False)

        lax.fori_loop(first + 1, (odd + 1) * per, single, 0)

    lane = lax.broadcasted_iota(jnp.int32, (BLOCK_ROWS, LANES), 1)
    sums = jnp.zeros((BLOCK_ROWS, LANES), jnp.float32)
    for head in range(q_heads):
        cols = slice(head * HEAD_DIMENSION, (head + 1) * HEAD_DIMENSION)
        out[:BLOCK_ROWS, cols] = acc[head, :, :HEAD_DIMENSION].astype(jnp.bfloat16)
        t = acc[head, :, HEAD_DIMENSION:]
        high = t.astype(jnp.bfloat16).astype(jnp.float32)
        sums = jnp.where(lane == head, high, jnp.where(lane == head + q_heads, t - high, sums))
    sums = jnp.transpose(sums).astype(jnp.bfloat16)
    groups = [sums[k * NOTE_ROWS : (k + 1) * NOTE_ROWS] for k in range(-(-2 * q_heads // NOTE_ROWS))]
    rest = out.shape[1] - len(groups) * BLOCK_ROWS
    out[BLOCK_ROWS:, :] = jnp.concatenate(groups + [jnp.zeros((NOTE_ROWS, rest), jnp.bfloat16)], axis=1)


def cut_kernel(query, piece, sem):
    copy = pltpu.make_async_copy(query.at[:, : piece.shape[1]], piece, sem)
    copy.start()
    copy.wait()


def pack_kernel(spans, other, dirty, keys, values, query, piece, tail, note, sem):
    rows = keys.shape[0]
    reach = (tail.shape[0] - NOTE_ROWS) // 2
    copies = [
        (query.at[:, query.shape[1] - piece.shape[1] :], piece),
        (keys.at[rows - reach :], tail.at[:reach]),
        (values.at[rows - reach :], tail.at[reach : 2 * reach]),
    ]
    copies = [pltpu.make_async_copy(a, b, sem.at[k]) for k, (a, b) in enumerate(copies)]
    for copy in copies:
        copy.start()
    mine = [lax.rem(spans[0, 0], rows), spans[0, 1] - spans[0, 0]]
    write_note(tail, mine)
    others = [lax.rem(other[0, 0], rows), other[0, 1] - other[0, 0]]
    for k, number in enumerate(mine + others + [dirty[0] + 1]):
        note[k] = number
    for k in range(5, note.shape[0]):
        note[k] = 0
    for copy in copies:
        copy.wait()


def chip_spans(index, rows, spans, other):
    mine = [lax.rem(spans[0, 0], rows), spans[0, 1] - spans[0, 0]]
    others = [lax.rem(other[0, 0], rows), other[0, 1] - other[0, 0]]
    return by_parity(lax.rem(index, 2), mine, others)


def prepare_kernel(
    index_ref, spans, other, angles, freq, k_own, k_other, v_own, v_other, kr, vz, lv, kb, vb, waves, sem,
):
    rows = k_own.shape[0]
    per = rows // BLOCK_ROWS
    kv_heads = kr.shape[0]
    index = index_ref[0]
    odd = lax.rem(index, 2)

    def copies(i, pair):
        into = pl.ds(pl.multiple_of(i * BLOCK_ROWS, BLOCK_ROWS), BLOCK_ROWS)
        t = lax.rem(i, per)
        of = pl.ds(pl.multiple_of(t * BLOCK_ROWS, BLOCK_ROWS), BLOCK_ROWS)
        return [
            pltpu.make_async_copy(ref.at[of, :], buf.at[into, :], sem.at[k, i])
            for k, (ref, buf) in enumerate(zip(pair, (kb, vb)))
        ]

    for i in range(2 * per):
        for copy in copies(i, (k_own, v_own) if i < per else (k_other, v_other)):
            copy.start()
    frame = Frame(dict(enumerate(chip_spans(index, rows, spans, other))), rows)
    tiles = [frame.tile(s, t * BLOCK_ROWS) for s in (0, 1) for t in range(per)]
    waves[0], waves[1] = wave([o for tile in tiles for o in tile[:2]], freq[...])
    row = lax.broadcasted_iota(jnp.int32, (BLOCK_ROWS, LANES), 0)

    def one(i, carry):
        for copy in copies(i, (k_own, v_own)):
            copy.wait()
        shard = jnp.where(i < per, odd, 1 - odd)
        t = lax.rem(i, per)
        at = shard * per + t
        tile = [
            jnp.where(shard == 1, b, a)
            for a, b in zip(*[frame.tile(s, t * BLOCK_ROWS) for s in (0, 1)])
        ]
        rows_of = (waves[0, pl.ds(2 * at, 2), :], waves[1, pl.ds(2 * at, 2), :])
        c, s = rope_tables(angles, tile[2], rows_of, 0, 1.0)
        live = jnp.where((row < tile[2]) | (row >= tile[3]), 1.0, 0.0).astype(jnp.bfloat16)
        into = pl.ds(pl.multiple_of(at * BLOCK_ROWS, BLOCK_ROWS), BLOCK_ROWS)
        of = pl.ds(pl.multiple_of(i * BLOCK_ROWS, BLOCK_ROWS), BLOCK_ROWS)
        lv[into, :] = live
        for h in range(kv_heads):
            cols = slice(h * HEAD_DIMENSION, (h + 1) * HEAD_DIMENSION)
            kr[h, into, :] = rotate(kb[of, cols], c, s)
            vz[h, into, :] = vb[of, cols] * live
        return carry

    lax.fori_loop(0, 2 * per, one, 0)


def visit_kernel(kind, step, shards, rows, low, index_ref, spans, other, dirty, *refs):
    index = index_ref[0]
    odd = lax.rem(index, 2)
    held = dict(enumerate(chip_spans(index, rows, spans, other)))
    block = dirty[0]
    through = lax.rem(index // 2, 2) == 1
    if kind == "window":
        near_note, note, tail, *refs = refs
        held[2] = (0, near_note[1] + near_note[3])
        held[3] = (0, 0)
    elif kind == "middle":
        note, direct, relayed, *refs = refs
    if kind != "own":
        held[step], held[step + 1] = by_parity(odd, (note[0], note[1]), (note[2], note[3]))
        block = note[4] - 1
    angles, freq, kr, vz, lv, *refs = refs
    if kind == "middle":

        def query(cols):
            a = direct[:BLOCK_ROWS, cols].astype(jnp.float32)
            return jnp.where(through, relayed[:BLOCK_ROWS, cols].astype(jnp.float32), a)
    else:
        queries, *refs = refs
        query = lambda cols: queries[:BLOCK_ROWS, cols]
    out, *scratch = refs
    valid = (index + step < shards) & (block >= 0)

    @pl.when(jnp.logical_not(valid))
    def _():
        out[...] = jnp.zeros(out.shape, out.dtype)

    @pl.when(valid)
    def _():
        edge = {"block": (step, step + 1)}
        if kind == "window":
            held[-1] = read_note(tail[tail.shape[0] - NOTE_ROWS :, :LANES], 2)
            reach = (tail.shape[0] - NOTE_ROWS) // 2
            tail_tile = Frame(held, rows).tile(-1, rows - BLOCK_ROWS)
            edge["tail"] = tail.at[:reach, :], tail.at[reach : 2 * reach, :], tail_tile
        frame = Frame(held, rows)
        keys = (kr, vz, lv)
        visit(kind, index, block, frame, freq[...], angles, low, query, keys, edge, out, scratch)


def last_kernel(rows, low, spans, dirty, index_ref, own, a, b, *refs):
    out, result, sem = refs[-3:]
    index = index_ref[0]
    heads = result.shape[1] // HEAD_DIMENSION
    block = dirty[0]
    first = index * rows + jnp.maximum(block, 0) * BLOCK_ROWS
    row = lax.broadcasted_iota(jnp.int32, (BLOCK_ROWS, LANES), 0) + first
    keep = ((row < spans[0, 0]) | (row >= spans[0, 1])) & (block >= 0)
    rows_of, heads_of = [], []
    for ref, count, lowest in ((own, own.shape[1] // HEAD_DIMENSION, 0), (a, heads, low), (b, heads, low)):
        for k in range(-(-2 * count // NOTE_ROWS)):
            rows_of.append(ref[BLOCK_ROWS:, k * BLOCK_ROWS : (k + 1) * BLOCK_ROWS].astype(jnp.float32))
            for r in range(k * NOTE_ROWS, (k + 1) * NOTE_ROWS):
                heads_of.append(lowest + r % count if r < 2 * count else -1)
    rows_of.append(jnp.zeros((LANES - len(heads_of), BLOCK_ROWS), jnp.float32))
    totals = jnp.transpose(jnp.concatenate(rows_of, axis=0)).astype(jnp.bfloat16)
    line = lax.broadcasted_iota(jnp.int32, (LANES, LANES), 0)
    for head in range(heads):
        hit = [line == r for r, h in enumerate(heads_of) if h == low + head]
        pick = jnp.where(functools.reduce(jnp.logical_or, hit), 1.0, 0.0).astype(jnp.bfloat16)
        total = jnp.dot(totals, pick, preferred_element_type=jnp.float32)
        total = jnp.where(total > 0, total, 1.0)
        cols = slice(head * HEAD_DIMENSION, (head + 1) * HEAD_DIMENSION)
        from_own = slice(cols.start + low * HEAD_DIMENSION, cols.stop + low * HEAD_DIMENSION)
        number = (
            own[:BLOCK_ROWS, from_own].astype(jnp.float32)
            + a[:BLOCK_ROWS, cols].astype(jnp.float32)
            + b[:BLOCK_ROWS, cols].astype(jnp.float32)
        )
        result[:, cols] = jnp.where(keep, number / total, 0.0).astype(result.dtype)
    copy = pltpu.make_async_copy(
        result, out.at[:, low * HEAD_DIMENSION : (low + heads) * HEAD_DIMENSION], sem
    )
    copy.start()
    copy.wait()


SMEM = pl.BlockSpec(memory_space=pltpu.SMEM)
VMEM = pl.BlockSpec(memory_space=pltpu.VMEM)
HBM = pl.BlockSpec(memory_space=pltpu.HBM)


def in_hbm(array):
    return pltpu.with_memory_space_constraint(array, pltpu.HBM)


def work(queries, keys, values, dirty, spans):
    shards = lax.axis_size("seq")
    index = lax.axis_index("seq")
    rows, columns = keys.shape
    kv_heads = columns // HEAD_DIMENSION
    per = rows // BLOCK_ROWS
    back = WINDOW // rows
    reach = (back + 1) * SPAN
    swap = [(i, i ^ 1) for i in range(shards)]
    onward = [(i, i + 1) for i in range(1, shards - 1, 2)]

    second = kv_heads * SECOND_PART // 8
    parts = [(0, kv_heads - second), (kv_heads - second, second)]
    params = pltpu.CompilerParams(vmem_limit_bytes=VMEM_LIMIT)

    other = send(spans, swap)
    k_other = send(keys, swap)
    v_other = send(values, swap)
    widths = [2 * heads * HEAD_DIMENSION for _, heads in parts]
    piece = pl.pallas_call(
        cut_kernel,
        out_shape=jax.ShapeDtypeStruct((BLOCK_ROWS, widths[0]), queries.dtype),
        in_specs=[HBM],
        out_specs=VMEM,
        scratch_shapes=[pltpu.SemaphoreType.DMA(())],
        compiler_params=params,
        cost_estimate=pl.CostEstimate(flops=1, bytes_accessed=1 << 20, transcendentals=0),
        name="cut",
    )(in_hbm(queries))
    rest, tail, note = pl.pallas_call(
        pack_kernel,
        out_shape=[
            jax.ShapeDtypeStruct((BLOCK_ROWS, widths[1]), queries.dtype),
            jax.ShapeDtypeStruct((2 * reach + NOTE_ROWS, columns), keys.dtype),
            jax.ShapeDtypeStruct((8,), jnp.int32),
        ],
        in_specs=[SMEM] * 3 + [HBM] * 3,
        out_specs=[VMEM] * 2 + [SMEM],
        scratch_shapes=[pltpu.SemaphoreType.DMA((3,))],
        compiler_params=params,
        cost_estimate=pl.CostEstimate(flops=1, bytes_accessed=2 << 20, transcendentals=0),
        name="pack",
    )(spans, other, dirty, in_hbm(keys), in_hbm(values), in_hbm(queries))
    pieces = [piece, rest]
    odd_to_even = [(i, i - back // 2) for i in range(shards) if i // 2 % 2 == 1]
    even_to_odd = [(i, i + back // 2) for i in range(shards - back // 2) if i // 2 % 2 == 0]
    far = [shift(piece, -back) for piece in pieces]
    near = [send(piece, odd_to_even) for piece in pieces]
    relay = [send(piece, even_to_odd) for piece in far]
    tail = send(tail, onward)
    near_note = shift(note, -back // 2)
    far_note = shift(note, -back)

    at = index.astype(jnp.int32).reshape(1)
    angles = jnp.asarray(row_angles())
    freq = jnp.asarray(lane_frequency()[None, :])

    def payload(heads):
        return jax.ShapeDtypeStruct((BLOCK_ROWS + NOTE_ROWS, heads * HEAD_DIMENSION), jnp.bfloat16)

    by_head = pltpu.VMEM((kv_heads, 2 * rows, HEAD_DIMENSION), jnp.bfloat16)
    kr, vz, lv = pl.pallas_call(
        prepare_kernel,
        out_shape=(by_head, by_head, pltpu.VMEM((2 * rows, LANES), jnp.bfloat16)),
        in_specs=[SMEM] * 3 + [VMEM] * 2 + [HBM] * 4,
        out_specs=[VMEM] * 3,
        scratch_shapes=[
            pltpu.VMEM((2 * rows, columns), keys.dtype),
            pltpu.VMEM((2 * rows, columns), keys.dtype),
            pltpu.VMEM((2, -(-4 * per // 8) * 8, LANES), jnp.float32),
            pltpu.SemaphoreType.DMA((2, 2 * per)),
        ],
        compiler_params=params,
        cost_estimate=pl.CostEstimate(flops=1 << 24, bytes_accessed=20 << 20, transcendentals=0),
        name="prepare",
    )(at, spans, other, angles, freq, *map(in_hbm, (keys, k_other, values, v_other)))

    def visitor(kind, step, part, small, notes, query):
        low, heads = (0, kv_heads) if part is None else parts[part]
        count = {"own": per, "middle": 2 * per, "window": per}[kind] * BLOCK_ROWS
        work = BLOCK_ROWS * 2 * heads * count
        edges = {"own": 1, "middle": 1, "window": 2}[kind]
        return pl.pallas_call(
            functools.partial(visit_kernel, kind, step, shards, rows, low),
            out_shape=payload(2 * heads),
            in_specs=[SMEM] * (4 + len(small)) + [VMEM] * (5 + len(notes) + len(query)),
            out_specs=VMEM,
            scratch_shapes=[
                pltpu.VMEM((2 * heads, BLOCK_ROWS, HEAD_DIMENSION), jnp.bfloat16),
                pltpu.VMEM((2 * heads, BLOCK_ROWS, HEAD_DIMENSION + LANES), jnp.float32),
                pltpu.VMEM((edges, heads, BLOCK_ROWS, HEAD_DIMENSION), jnp.bfloat16),
                pltpu.VMEM((edges, heads, BLOCK_ROWS, HEAD_DIMENSION), jnp.bfloat16),
                pltpu.VMEM((edges, BLOCK_ROWS, LANES), jnp.bfloat16),
            ],
            compiler_params=params,
            cost_estimate=pl.CostEstimate(
                flops=work * 4 * HEAD_DIMENSION, bytes_accessed=6 << 20, transcendentals=2 * work
            ),
        )(at, spans, other, dirty, *small, *notes, angles, freq, kr, vz, lv, *query)

    middle, window = [], []
    for p in range(len(parts)):
        got = visitor("window", back, p, [near_note, far_note], [tail], [far[p]])
        window.append(shift(got, back))
        got = visitor("middle", back // 2, p, [near_note], [near[p], relay[p]], [])
        middle.append(shift(got, back // 2))
    own = visitor("own", 0, None, [], [], [queries])
    result = []
    for (low, heads), a, b in zip(parts, middle, window):
        result = [
            pl.pallas_call(
                functools.partial(last_kernel, rows, 2 * low),
                out_shape=jax.ShapeDtypeStruct(queries.shape, queries.dtype),
                in_specs=[SMEM] * 3 + [VMEM] * 3 + [HBM] * len(result),
                out_specs=HBM,
                scratch_shapes=[
                    pltpu.VMEM((BLOCK_ROWS, 2 * heads * HEAD_DIMENSION), queries.dtype),
                    pltpu.SemaphoreType.DMA(()),
                ],
                input_output_aliases={6: 0} if result else {},
                compiler_params=params,
                name="last",
            )(spans, dirty, at, own, a, b, *result)
        ]
    return result[0]


def solution(mesh):
    placed = (
        P(("groups", "seq"), None),
        P(("groups", "seq"), None),
        P(("groups", "seq"), None),
        P(("groups", "seq")),
        P(("groups", "seq"), None),
    )
    return jax.shard_map(
        work, mesh=mesh, in_specs=placed, out_specs=P(("groups", "seq"), None), check_vma=False
    )
```

```python
import functools
import math

import jax
import jax.numpy as jnp
import numpy as np
from jax import lax
from jax.experimental import pallas as pl
from jax.experimental.pallas import tpu as pltpu
from jax.sharding import PartitionSpec as P


HEAD_DIMENSION = 128
WINDOW = 4096
BLOCK_ROWS = 256
SPAN = 32

SOFTCAP = 50.0
QUERY_SCALE = 144.0 ** (-0.5)
TO_TANH = 1.0 / SOFTCAP
TO_EXP2 = SOFTCAP * math.log2(math.e)

HALF = HEAD_DIMENSION // 2
LANES = 128
NOTE_ROWS = 8
SECOND_PART = 3
DIGIT = 32
VMEM_LIMIT = 32 << 20


def lane_frequency():
    order = np.arange(HEAD_DIMENSION) % HALF
    return np.exp(order * (-2.0 * math.log(10000.0) / HEAD_DIMENSION)).astype(np.float32)


def row_angles():
    angle = np.arange(BLOCK_ROWS, dtype=np.float64)[:, None] * lane_frequency().astype(np.float64)[None, :]
    sign = np.where(np.arange(HEAD_DIMENSION) < HALF, -1.0, 1.0)[None, :]
    return np.stack([np.cos(angle), np.sin(angle) * sign]).astype(np.float32)


def send(array, pairs):
    return lax.ppermute(array, "seq", pairs)


def shift(array, by):
    count = lax.axis_size("seq")
    return send(array, [(i, i + by) for i in range(count) if 0 <= i + by < count])


class Frame:
    def __init__(self, spans, rows):
        self.spans, self.rows = spans, rows

    def tile(self, shard_step, row):
        start, length = self.spans[shard_step]
        first = shard_step * self.rows + row
        for step in range(min(shard_step, 0), max(shard_step, 0)):
            _, other = self.spans[step]
            first = first - other if step >= 0 else first + other
        first = first - jnp.clip(row - start, 0, length)
        begin = start - row
        end = begin + length
        gone = jnp.clip(end, 0, BLOCK_ROWS) - jnp.clip(begin, 0, BLOCK_ROWS)
        return first, first - gone, begin, end


def by_parity(odd, mine, other):
    mine = [jnp.where(odd == 1, b, a) for a, b in zip(mine, other)], [
        jnp.where(odd == 1, a, b) for a, b in zip(mine, other)
    ]
    return mine


def write_note(ref, numbers):
    shape = (NOTE_ROWS, ref.shape[1])
    lane = lax.broadcasted_iota(jnp.int32, shape, 1)
    row = jnp.zeros(shape, jnp.int32)
    for k, number in enumerate(numbers):
        row = jnp.where(lane == 2 * k, number // DIGIT, jnp.where(lane == 2 * k + 1, number % DIGIT, row))
    ref[ref.shape[0] - NOTE_ROWS :, :] = row.astype(jnp.float32).astype(jnp.bfloat16)


def read_note(note, count):
    low = note.astype(jnp.float32)
    shape = (NOTE_ROWS, LANES)
    lane = lax.broadcasted_iota(jnp.int32, shape, 1)
    first = lax.broadcasted_iota(jnp.int32, shape, 0) == 0
    out = []
    for k in range(count):
        digits = jnp.where(lane == 2 * k, low * DIGIT, jnp.where(lane == 2 * k + 1, low, 0.0))
        out.append(jnp.sum(jnp.where(first, digits, 0.0)).astype(jnp.int32))
    return out


def wave(offsets, freq):
    count = -(-len(offsets) // 8) * 8
    row = lax.broadcasted_iota(jnp.int32, (count, LANES), 0)
    lane = lax.broadcasted_iota(jnp.int32, (count, LANES), 1)
    value = jnp.zeros((count, LANES), jnp.int32)
    for k, offset in enumerate(offsets):
        value = jnp.where(row == k, offset, value)
    angle = value.astype(jnp.float32) * freq
    sine = jnp.sin(angle)
    return jnp.cos(angle), jnp.where(lane < HALF, -sine, sine)


def rope_tables(angles, begin, waves, at, scale):
    cosine, sine = waves
    row = lax.broadcasted_iota(jnp.int32, (BLOCK_ROWS, LANES), 0)
    early = row < begin
    c = jnp.where(early, cosine[at : at + 1], cosine[at + 1 : at + 2])
    s = jnp.where(early, sine[at : at + 1], sine[at + 1 : at + 2])
    rc, rs = angles[0], angles[1]
    return (rc * c - rs * s) * scale, (rs * c + rc * s) * scale


def rotate(x, c, s):
    x = x.astype(jnp.float32)
    return (x * c + pltpu.roll(x, HALF, 1) * s).astype(jnp.bfloat16)


def places(tile, dim, shape):
    first, later, begin, _ = tile
    row = lax.broadcasted_iota(jnp.int32, shape, dim)
    return row + jnp.where(row < begin, first, later)


def visit(kind, index, block, frame, freq, angles, low, query, keys, edge, out, scratch):
    kr, vz, lv = keys
    rot, acc, ke, ve, le = scratch
    odd = lax.rem(index, 2)
    per = frame.rows // BLOCK_ROWS
    q_heads = acc.shape[0]
    kv_heads = q_heads // 2
    pair = [frame.tile(s, block * BLOCK_ROWS) for s in edge["block"]]
    tile = [jnp.where(odd == 1, b, a) for a, b in zip(*pair)]
    waves = wave([tile[0], tile[1]], freq)
    c, s = rope_tables(angles, tile[2], waves, 0, QUERY_SCALE)
    for head in range(q_heads):
        cols = slice(head * HEAD_DIMENSION, (head + 1) * HEAD_DIMENSION)
        rot[head] = rotate(query(cols), c, s)
    own = places(tile, 0, (BLOCK_ROWS, 1))

    def add(head, keys_of, values_of, keep, fresh):
        score = lax.dot_general(
            rot[head], keys_of, (((1,), (1,)), ((), ())), preferred_element_type=jnp.float32
        )
        weight = jnp.exp2(jnp.tanh(score * TO_TANH) * TO_EXP2)
        if keep is not None:
            weight = jnp.where(keep, weight, 0.0)
        both = jnp.dot(weight.astype(jnp.bfloat16), values_of, preferred_element_type=jnp.float32)
        acc[head] = both if fresh else acc[head] + both

    def many(begin, count, fresh):
        some = pl.ds(pl.multiple_of(begin * BLOCK_ROWS, BLOCK_ROWS), count * BLOCK_ROWS)

        def one(i, carry):
            v = jnp.concatenate([vz[low + i, some, :], lv[some, :]], axis=1)
            for g in range(2):
                add(2 * i + g, kr[low + i, some, :], v, None, fresh)
            return carry

        lax.fori_loop(0, kv_heads, one, 0)

    def single(at, carry):
        some = pl.ds(pl.multiple_of(at * BLOCK_ROWS, BLOCK_ROWS), BLOCK_ROWS)
        live = lv[some, :]
        for i in range(kv_heads):
            v = jnp.concatenate([vz[low + i, some, :], live], axis=1)
            for g in range(2):
                add(2 * i + g, kr[low + i, some, :], v, None, False)
        return carry

    def stage(slot, at):
        some = pl.ds(pl.multiple_of(at * BLOCK_ROWS, BLOCK_ROWS), BLOCK_ROWS)
        into = slice(slot * BLOCK_ROWS, (slot + 1) * BLOCK_ROWS)
        for i in range(kv_heads):
            ke[i, into] = kr[low + i, some, :]
            ve[i, into] = vz[low + i, some, :]
        le[into] = lv[some, :]

    def masked(keep):
        for i in range(kv_heads):
            v = jnp.concatenate([ve[i], le[...]], axis=1)
            for g in range(2):
                add(2 * i + g, ke[i], v, keep, True)

    def places_at(at):
        pair = [frame.tile(s, at * BLOCK_ROWS) for s in (0, 1)]
        tile = [jnp.where(odd == 1, b, a) for a, b in zip(*pair)]
        return places(tile, 1, (1, BLOCK_ROWS))

    if kind == "middle":
        many(0, 2 * per, True)
    elif kind == "own":
        stage(0, odd * per + block)
        masked(own >= places_at(block))

        @pl.when(odd == 1)
        def _():
            many(0, per, False)

        lax.fori_loop(odd * per, odd * per + block, single, 0)
    else:
        first = odd * per + block
        tail_k, tail_v, tail_tile = edge["tail"]

        @pl.when(first > 0)
        def _():
            stage(0, first - 1)

        @pl.when(first == 0)
        def _():
            reach = tail_k.shape[0]
            row = lax.broadcasted_iota(jnp.int32, (BLOCK_ROWS, LANES), 0)
            live = (row < tail_tile[2]) | (row >= tail_tile[3])
            live = live & (row >= BLOCK_ROWS - reach) & (index > 0)
            c, s = rope_tables(angles, tail_tile[2], wave(list(tail_tile[:2]), freq), 0, 1.0)
            alive = jnp.where(live, 1.0, 0.0).astype(jnp.bfloat16)
            le[:BLOCK_ROWS] = alive
            zero = jnp.zeros((BLOCK_ROWS - reach, HEAD_DIMENSION), jnp.bfloat16)
            for i in range(kv_heads):
                cols = slice((low + i) * HEAD_DIMENSION, (low + i + 1) * HEAD_DIMENSION)
                ke[i, :BLOCK_ROWS] = rotate(jnp.concatenate([zero, tail_k[:, cols]], axis=0), c, s)
                ve[i, :BLOCK_ROWS] = jnp.concatenate([zero, tail_v[:, cols]], axis=0) * alive

        stage(1, first)
        inside = block > 0
        row = jnp.where(inside, block - 1, per - 1) * BLOCK_ROWS
        last = frame.tile(0, (per - 1) * BLOCK_ROWS)
        even = [jnp.where(inside, a, b) for a, b in zip(frame.tile(0, row), tail_tile)]
        other = [jnp.where(inside, a, b) for a, b in zip(frame.tile(1, row), last)]
        tile = [jnp.where(odd == 1, b, a) for a, b in zip(even, other)]
        before = places(tile, 1, (1, BLOCK_ROWS))
        masked(own - jnp.concatenate([before, places_at(block)], axis=1) < WINDOW)

        @pl.when(odd == 0)
        def _():
            many(per, per, False)

        lax.fori_loop(first + 1, (odd + 1) * per, single, 0)

    lane = lax.broadcasted_iota(jnp.int32, (BLOCK_ROWS, LANES), 1)
    sums = jnp.zeros((BLOCK_ROWS, LANES), jnp.float32)
    for head in range(q_heads):
        cols = slice(head * HEAD_DIMENSION, (head + 1) * HEAD_DIMENSION)
        out[:BLOCK_ROWS, cols] = acc[head, :, :HEAD_DIMENSION].astype(jnp.bfloat16)
        t = acc[head, :, HEAD_DIMENSION:]
        high = t.astype(jnp.bfloat16).astype(jnp.float32)
        sums = jnp.where(lane == head, high, jnp.where(lane == head + q_heads, t - high, sums))
    sums = jnp.transpose(sums).astype(jnp.bfloat16)
    groups = [sums[k * NOTE_ROWS : (k + 1) * NOTE_ROWS] for k in range(-(-2 * q_heads // NOTE_ROWS))]
    rest = out.shape[1] - len(groups) * BLOCK_ROWS
    out[BLOCK_ROWS:, :] = jnp.concatenate(groups + [jnp.zeros((NOTE_ROWS, rest), jnp.bfloat16)], axis=1)


def cut_kernel(query, piece, sem):
    copy = pltpu.make_async_copy(query.at[:, : piece.shape[1]], piece, sem)
    copy.start()
    copy.wait()


def pack_kernel(spans, other, dirty, keys, values, query, piece, tail, note, sem):
    rows = keys.shape[0]
    reach = (tail.shape[0] - NOTE_ROWS) // 2
    copies = [
        (query.at[:, query.shape[1] - piece.shape[1] :], piece),
        (keys.at[rows - reach :], tail.at[:reach]),
        (values.at[rows - reach :], tail.at[reach : 2 * reach]),
    ]
    copies = [pltpu.make_async_copy(a, b, sem.at[k]) for k, (a, b) in enumerate(copies)]
    for copy in copies:
        copy.start()
    mine = [lax.rem(spans[0, 0], rows), spans[0, 1] - spans[0, 0]]
    write_note(tail, mine)
    others = [lax.rem(other[0, 0], rows), other[0, 1] - other[0, 0]]
    for k, number in enumerate(mine + others + [dirty[0] + 1]):
        note[k] = number
    for k in range(5, note.shape[0]):
        note[k] = 0
    for copy in copies:
        copy.wait()


def chip_spans(index, rows, spans, other):
    mine = [lax.rem(spans[0, 0], rows), spans[0, 1] - spans[0, 0]]
    others = [lax.rem(other[0, 0], rows), other[0, 1] - other[0, 0]]
    return by_parity(lax.rem(index, 2), mine, others)


def prepare_kernel(
    index_ref, spans, other, angles, freq, k_own, k_other, v_own, v_other, kr, vz, lv, kb, vb, waves, sem,
):
    rows = k_own.shape[0]
    per = rows // BLOCK_ROWS
    kv_heads = kr.shape[0]
    index = index_ref[0]
    odd = lax.rem(index, 2)

    def copies(i, pair):
        into = pl.ds(pl.multiple_of(i * BLOCK_ROWS, BLOCK_ROWS), BLOCK_ROWS)
        t = lax.rem(i, per)
        of = pl.ds(pl.multiple_of(t * BLOCK_ROWS, BLOCK_ROWS), BLOCK_ROWS)
        return [
            pltpu.make_async_copy(ref.at[of, :], buf.at[into, :], sem.at[k, i])
            for k, (ref, buf) in enumerate(zip(pair, (kb, vb)))
        ]

    for i in range(2 * per):
        for copy in copies(i, (k_own, v_own) if i < per else (k_other, v_other)):
            copy.start()
    frame = Frame(dict(enumerate(chip_spans(index, rows, spans, other))), rows)
    tiles = [frame.tile(s, t * BLOCK_ROWS) for s in (0, 1) for t in range(per)]
    waves[0], waves[1] = wave([o for tile in tiles for o in tile[:2]], freq[...])
    row = lax.broadcasted_iota(jnp.int32, (BLOCK_ROWS, LANES), 0)

    def one(i, carry):
        for copy in copies(i, (k_own, v_own)):
            copy.wait()
        shard = jnp.where(i < per, odd, 1 - odd)
        t = lax.rem(i, per)
        at = shard * per + t
        tile = [
            jnp.where(shard == 1, b, a)
            for a, b in zip(*[frame.tile(s, t * BLOCK_ROWS) for s in (0, 1)])
        ]
        rows_of = (waves[0, pl.ds(2 * at, 2), :], waves[1, pl.ds(2 * at, 2), :])
        c, s = rope_tables(angles, tile[2], rows_of, 0, 1.0)
        live = jnp.where((row < tile[2]) | (row >= tile[3]), 1.0, 0.0).astype(jnp.bfloat16)
        into = pl.ds(pl.multiple_of(at * BLOCK_ROWS, BLOCK_ROWS), BLOCK_ROWS)
        of = pl.ds(pl.multiple_of(i * BLOCK_ROWS, BLOCK_ROWS), BLOCK_ROWS)
        lv[into, :] = live
        for h in range(kv_heads):
            cols = slice(h * HEAD_DIMENSION, (h + 1) * HEAD_DIMENSION)
            kr[h, into, :] = rotate(kb[of, cols], c, s)
            vz[h, into, :] = vb[of, cols] * live
        return carry

    lax.fori_loop(0, 2 * per, one, 0)


def visit_kernel(kind, step, shards, rows, low, index_ref, spans, other, dirty, *refs):
    index = index_ref[0]
    odd = lax.rem(index, 2)
    held = dict(enumerate(chip_spans(index, rows, spans, other)))
    block = dirty[0]
    through = lax.rem(index // 2, 2) == 1
    if kind == "window":
        near_note, note, tail, *refs = refs
        held[2] = (0, near_note[1] + near_note[3])
        held[3] = (0, 0)
    elif kind == "middle":
        note, direct, relayed, *refs = refs
    if kind != "own":
        held[step], held[step + 1] = by_parity(odd, (note[0], note[1]), (note[2], note[3]))
        block = note[4] - 1
    angles, freq, kr, vz, lv, *refs = refs
    if kind == "middle":

        def query(cols):
            a = direct[:BLOCK_ROWS, cols].astype(jnp.float32)
            return jnp.where(through, relayed[:BLOCK_ROWS, cols].astype(jnp.float32), a)
    else:
        queries, *refs = refs
        query = lambda cols: queries[:BLOCK_ROWS, cols]
    out, *scratch = refs
    valid = (index + step < shards) & (block >= 0)

    @pl.when(jnp.logical_not(valid))
    def _():
        out[...] = jnp.zeros(out.shape, out.dtype)

    @pl.when(valid)
    def _():
        edge = {"block": (step, step + 1)}
        if kind == "window":
            held[-1] = read_note(tail[tail.shape[0] - NOTE_ROWS :, :LANES], 2)
            reach = (tail.shape[0] - NOTE_ROWS) // 2
            tail_tile = Frame(held, rows).tile(-1, rows - BLOCK_ROWS)
            edge["tail"] = tail.at[:reach, :], tail.at[reach : 2 * reach, :], tail_tile
        frame = Frame(held, rows)
        keys = (kr, vz, lv)
        visit(kind, index, block, frame, freq[...], angles, low, query, keys, edge, out, scratch)


def last_kernel(rows, low, spans, dirty, index_ref, own, a, b, *refs):
    out, result, sem = refs[-3:]
    index = index_ref[0]
    heads = result.shape[0]
    copies = []
    block = dirty[0]
    first = index * rows + jnp.maximum(block, 0) * BLOCK_ROWS
    row = lax.broadcasted_iota(jnp.int32, (BLOCK_ROWS, LANES), 0) + first
    keep = ((row < spans[0, 0]) | (row >= spans[0, 1])) & (block >= 0)
    rows_of, heads_of = [], []
    for ref, count, lowest in ((own, own.shape[1] // HEAD_DIMENSION, 0), (a, heads, low), (b, heads, low)):
        for k in range(-(-2 * count // NOTE_ROWS)):
            rows_of.append(ref[BLOCK_ROWS:, k * BLOCK_ROWS : (k + 1) * BLOCK_ROWS].astype(jnp.float32))
            for r in range(k * NOTE_ROWS, (k + 1) * NOTE_ROWS):
                heads_of.append(lowest + r % count if r < 2 * count else -1)
    rows_of.append(jnp.zeros((LANES - len(heads_of), BLOCK_ROWS), jnp.float32))
    totals = jnp.transpose(jnp.concatenate(rows_of, axis=0)).astype(jnp.bfloat16)
    line = lax.broadcasted_iota(jnp.int32, (LANES, LANES), 0)
    for head in range(heads):
        hit = [line == r for r, h in enumerate(heads_of) if h == low + head]
        pick = jnp.where(functools.reduce(jnp.logical_or, hit), 1.0, 0.0).astype(jnp.bfloat16)
        total = jnp.dot(totals, pick, preferred_element_type=jnp.float32)
        total = jnp.where(total > 0, total, 1.0)
        cols = slice(head * HEAD_DIMENSION, (head + 1) * HEAD_DIMENSION)
        from_own = slice(cols.start + low * HEAD_DIMENSION, cols.stop + low * HEAD_DIMENSION)
        number = (
            own[:BLOCK_ROWS, from_own].astype(jnp.float32)
            + a[:BLOCK_ROWS, cols].astype(jnp.float32)
            + b[:BLOCK_ROWS, cols].astype(jnp.float32)
        )
        result[head] = jnp.where(keep, number / total, 0.0).astype(result.dtype)
        copies.append(pltpu.make_async_copy(result.at[head], out.at[:, from_own], sem.at[head]))
        copies[-1].start()
    for copy in copies:
        copy.wait()


SMEM = pl.BlockSpec(memory_space=pltpu.SMEM)
VMEM = pl.BlockSpec(memory_space=pltpu.VMEM)
HBM = pl.BlockSpec(memory_space=pltpu.HBM)


def in_hbm(array):
    return pltpu.with_memory_space_constraint(array, pltpu.HBM)


def work(queries, keys, values, dirty, spans):
    shards = lax.axis_size("seq")
    index = lax.axis_index("seq")
    rows, columns = keys.shape
    kv_heads = columns // HEAD_DIMENSION
    per = rows // BLOCK_ROWS
    back = WINDOW // rows
    reach = (back + 1) * SPAN
    swap = [(i, i ^ 1) for i in range(shards)]
    onward = [(i, i + 1) for i in range(1, shards - 1, 2)]

    second = kv_heads * SECOND_PART // 8
    parts = [(0, kv_heads - second), (kv_heads - second, second)]
    params = pltpu.CompilerParams(vmem_limit_bytes=VMEM_LIMIT)

    other = send(spans, swap)
    k_other = send(keys, swap)
    v_other = send(values, swap)
    widths = [2 * heads * HEAD_DIMENSION for _, heads in parts]
    piece = pl.pallas_call(
        cut_kernel,
        out_shape=jax.ShapeDtypeStruct((BLOCK_ROWS, widths[0]), queries.dtype),
        in_specs=[HBM],
        out_specs=VMEM,
        scratch_shapes=[pltpu.SemaphoreType.DMA(())],
        compiler_params=params,
        cost_estimate=pl.CostEstimate(flops=1, bytes_accessed=1 << 20, transcendentals=0),
        name="cut",
    )(in_hbm(queries))
    rest, tail, note = pl.pallas_call(
        pack_kernel,
        out_shape=[
            jax.ShapeDtypeStruct((BLOCK_ROWS, widths[1]), queries.dtype),
            jax.ShapeDtypeStruct((2 * reach + NOTE_ROWS, columns), keys.dtype),
            jax.ShapeDtypeStruct((8,), jnp.int32),
        ],
        in_specs=[SMEM] * 3 + [HBM] * 3,
        out_specs=[VMEM] * 2 + [SMEM],
        scratch_shapes=[pltpu.SemaphoreType.DMA((3,))],
        compiler_params=params,
        cost_estimate=pl.CostEstimate(flops=1, bytes_accessed=2 << 20, transcendentals=0),
        name="pack",
    )(spans, other, dirty, in_hbm(keys), in_hbm(values), in_hbm(queries))
    pieces = [piece, rest]
    odd_to_even = [(i, i - back // 2) for i in range(shards) if i // 2 % 2 == 1]
    even_to_odd = [(i, i + back // 2) for i in range(shards - back // 2) if i // 2 % 2 == 0]
    far = [shift(piece, -back) for piece in pieces]
    near = [send(piece, odd_to_even) for piece in pieces]
    relay = [send(piece, even_to_odd) for piece in far]
    tail = send(tail, onward)
    near_note = shift(note, -back // 2)
    far_note = shift(note, -back)

    at = index.astype(jnp.int32).reshape(1)
    angles = jnp.asarray(row_angles())
    freq = jnp.asarray(lane_frequency()[None, :])

    def payload(heads):
        return jax.ShapeDtypeStruct((BLOCK_ROWS + NOTE_ROWS, heads * HEAD_DIMENSION), jnp.bfloat16)

    by_head = pltpu.VMEM((kv_heads, 2 * rows, HEAD_DIMENSION), jnp.bfloat16)
    kr, vz, lv = pl.pallas_call(
        prepare_kernel,
        out_shape=(by_head, by_head, pltpu.VMEM((2 * rows, LANES), jnp.bfloat16)),
        in_specs=[SMEM] * 3 + [VMEM] * 2 + [HBM] * 4,
        out_specs=[VMEM] * 3,
        scratch_shapes=[
            pltpu.VMEM((2 * rows, columns), keys.dtype),
            pltpu.VMEM((2 * rows, columns), keys.dtype),
            pltpu.VMEM((2, -(-4 * per // 8) * 8, LANES), jnp.float32),
            pltpu.SemaphoreType.DMA((2, 2 * per)),
        ],
        compiler_params=params,
        cost_estimate=pl.CostEstimate(flops=1 << 24, bytes_accessed=20 << 20, transcendentals=0),
        name="prepare",
    )(at, spans, other, angles, freq, *map(in_hbm, (keys, k_other, values, v_other)))

    def visitor(kind, step, part, small, notes, query):
        low, heads = (0, kv_heads) if part is None else parts[part]
        count = {"own": per, "middle": 2 * per, "window": per}[kind] * BLOCK_ROWS
        work = BLOCK_ROWS * 2 * heads * count
        edges = {"own": 1, "middle": 1, "window": 2}[kind]
        return pl.pallas_call(
            functools.partial(visit_kernel, kind, step, shards, rows, low),
            out_shape=payload(2 * heads),
            in_specs=[SMEM] * (4 + len(small)) + [VMEM] * (5 + len(notes) + len(query)),
            out_specs=VMEM,
            scratch_shapes=[
                pltpu.VMEM((2 * heads, BLOCK_ROWS, HEAD_DIMENSION), jnp.bfloat16),
                pltpu.VMEM((2 * heads, BLOCK_ROWS, HEAD_DIMENSION + LANES), jnp.float32),
                pltpu.VMEM((heads, edges * BLOCK_ROWS, HEAD_DIMENSION), jnp.bfloat16),
                pltpu.VMEM((heads, edges * BLOCK_ROWS, HEAD_DIMENSION), jnp.bfloat16),
                pltpu.VMEM((edges * BLOCK_ROWS, LANES), jnp.bfloat16),
            ],
            compiler_params=params,
            cost_estimate=pl.CostEstimate(
                flops=work * 4 * HEAD_DIMENSION, bytes_accessed=6 << 20, transcendentals=2 * work
            ),
        )(at, spans, other, dirty, *small, *notes, angles, freq, kr, vz, lv, *query)

    middle, window = [], []
    for p in range(len(parts)):
        got = visitor("window", back, p, [near_note, far_note], [tail], [far[p]])
        window.append(shift(got, back))
        got = visitor("middle", back // 2, p, [near_note], [near[p], relay[p]], [])
        middle.append(shift(got, back // 2))
    own = visitor("own", 0, None, [], [], [queries])
    result = []
    for (low, heads), a, b in zip(parts, middle, window):
        result = [
            pl.pallas_call(
                functools.partial(last_kernel, rows, 2 * low),
                out_shape=jax.ShapeDtypeStruct(queries.shape, queries.dtype),
                in_specs=[SMEM] * 3 + [VMEM] * 3 + [HBM] * len(result),
                out_specs=HBM,
                scratch_shapes=[
                    pltpu.VMEM((2 * heads, BLOCK_ROWS, HEAD_DIMENSION), queries.dtype),
                    pltpu.SemaphoreType.DMA((2 * heads,)),
                ],
                input_output_aliases={6: 0} if result else {},
                compiler_params=params,
                name="last",
            )(spans, dirty, at, own, a, b, *result)
        ]
    return result[0]


def solution(mesh):
    placed = (
        P(("groups", "seq"), None),
        P(("groups", "seq"), None),
        P(("groups", "seq"), None),
        P(("groups", "seq")),
        P(("groups", "seq"), None),
    )
    return jax.shard_map(
        work, mesh=mesh, in_specs=placed, out_specs=P(("groups", "seq"), None), check_vma=False
    )
```
